32 devices in a mesh: dp: 4 (over y, x), ctx: 8 (over z, core).
Axes of the slice: x: 2, y: 2, z: 4, core: 2. Of those that a mesh axis runs over, the one named last changes fastest.
Arguments:
- queries: bfloat16 [4, 1024, 2048], P('dp', 'ctx'), may hold values from -6 to 6
- key_rows: bfloat16 [4, 1024, 2048], P('dp', 'ctx'), may hold values from -6 to 6
- value_rows: bfloat16 [4, 1024, 2048], P('dp', 'ctx'), may hold values from -6 to 6
- out_cotangent: bfloat16 [4, 1024, 2048], P('dp', 'ctx'), may hold values from -12 to 12
- norm_gain: float32 [2048], replicated, may hold values from 0.1 to 1.9
- doc_starts: int32 [4, 4], P('dp'), may hold values from 0 to 7, as said below
Outputs:
- query_grad: bfloat16 [4, 1024, 2048], P('dp', 'ctx')
- key_grad: bfloat16 [4, 1024, 2048], P('dp', 'ctx')
- value_grad: bfloat16 [4, 1024, 2048], P('dp', 'ctx')
- gain_grad: float32 [2048], replicated
The draws below stay inside these ranges and needn't reach their ends.
Inputs may be any that keep to these rules, and one draw needn't show every extreme that they name: `doc_starts`: each row begins with 0 and rises strictly; entry d is the first block of 128 tokens of document d of that sequence, and the documents fill the sequence.
All inputs are finite; a program needn't handle non-finite values.
Results may differ from the reference program's by a relative error of at most 0.011.
Values sent between devices are 32-bit elements; how exact they have to be, the bound alone decides.
No kernel may reach another device: no remote copies, remote signals or barrier semaphores. Data moves between devices by JAX's collectives and lax.ppermute only.
A program may use at most 192 MiB of HBM per device.

```python
import jax
import jax.numpy as jnp
from jax import lax

H = 16
DH = 128
SPAN = 128
NDOC = 4
HD = 2048
SEQS = 4
LEN = 1024
NCHUNK = 8


def draw_out_cotangent(key, part):
    first = jax.random.fold_in(key, 21)
    values = jax.random.normal(first, (SEQS, LEN, HD), jnp.float32)
    values = jnp.clip(values, -4.0, 4.0)
    ramp = 1.0 + 2.0 * jnp.arange(LEN, dtype=jnp.float32) / (LEN - 1)
    return (values * ramp[None, :, None]).astype(jnp.bfloat16)


def draw_doc_starts(key, part):
    row_keys = jax.random.split(jax.random.fold_in(key, 11), SEQS)

    def one_row(row_key):
        picked = jax.random.permutation(row_key, NCHUNK - 1)[:NDOC - 1] + 1
        return jnp.sort(picked.astype(jnp.int32))
    inner = jax.vmap(one_row)(row_keys).astype(jnp.int32)
    chosen = jax.random.randint(jax.random.fold_in(key, 12), (), 0, SEQS)
    rows_index = jnp.arange(SEQS, dtype=jnp.int32)
    final = jnp.where(rows_index == chosen, jnp.int32(NCHUNK - 1), inner[:, -1])
    inner = inner.at[:, -1].set(final)
    return jnp.concatenate([jnp.zeros((SEQS, 1), jnp.int32), inner], axis=1)


def shard_levels(stream_key, dims, cuts, low, top_value):
    factor_of = 1.0
    for dim, parts in cuts:
        steps = jax.random.uniform(jax.random.fold_in(jax.random.fold_in(stream_key, 6), dim), (parts,), jnp.float32, low / len(cuts), top_value / len(cuts))
        factor_of = factor_of * jnp.repeat(jnp.exp(steps), dims[dim] // parts).reshape((-1,) + (1,) * (len(dims) - 1 - dim))
    return factor_of


def gaussian(key, extent, deviation, most, cuts=(), kind=jnp.bfloat16):
    loudness = shard_levels(key, extent, cuts, -0.22, 0.18) if cuts else 1.0
    drawn = jax.random.normal(key, extent, jnp.float32) * deviation * loudness
    return jnp.minimum(jnp.maximum(drawn, -most), most).astype(kind)


def setup_inputs(seed: int = 0) -> dict:
    streams_of = jax.random.split(jax.random.key(seed), 7)
    queries = gaussian(streams_of[0], (SEQS, LEN, HD), 1.0, 6.0, ((0, 4), (1, 8)))
    key_rows = gaussian(streams_of[1], (SEQS, LEN, HD), 1.0, 6.0, ((0, 4), (1, 8)))
    value_rows = gaussian(streams_of[2], (SEQS, LEN, HD), 1.0, 6.0, ((0, 4), (1, 8)))
    out_cotangent = draw_out_cotangent(jax.random.fold_in(streams_of[6], 71), 0)
    norm_gain = jnp.clip(1.0 + 0.18 * jax.random.normal(streams_of[4], (HD,), jnp.float32), 0.1, 1.9)
    doc_starts = draw_doc_starts(jax.random.fold_in(streams_of[6], 71), 0)
    return dict(queries=queries, key_rows=key_rows, value_rows=value_rows, out_cotangent=out_cotangent, norm_gain=norm_gain, doc_starts=doc_starts)


epsilon = 1e-06

def feature_map(x):
    wide = x.astype(jnp.float32)
    return jnp.where(wide > 0, wide + 1.0, jnp.exp(jnp.minimum(wide, 0.0)))

def feature_slope(x):
    wide = x.astype(jnp.float32)
    return jnp.where(wide > 0, 1.0, jnp.exp(jnp.minimum(wide, 0.0)))

def round_keep(x):
    return lax.optimization_barrier(x.astype(jnp.bfloat16)).astype(jnp.float32)

def reference(queries, key_rows, value_rows, out_cotangent, norm_gain, doc_starts):
    gain_heads = norm_gain.reshape(H, DH)

    def one_sequence(element):
        query_seq, key_seq, value_seq, cot_seq, starts = element
        length = query_seq.shape[0]
        blocks = length // SPAN
        query_feat = feature_map(query_seq).astype(jnp.bfloat16).astype(jnp.float32).reshape(blocks, SPAN, H, DH)
        key_feat = feature_map(key_seq).astype(jnp.bfloat16).astype(jnp.float32).reshape(blocks, SPAN, H, DH)
        value_four = value_seq.astype(jnp.float32).reshape(blocks, SPAN, H, DH)
        cot_four = cot_seq.astype(jnp.float32).reshape(blocks, SPAN, H, DH)
        flags = jnp.any(jnp.arange(blocks, dtype=jnp.int32)[:, None] == starts[None, :], axis=1)
        causal = jnp.tril(jnp.ones((SPAN, SPAN), jnp.float32))
        key_value = jnp.einsum('cthd,cthe->chde', key_feat, value_four)

        def forward_step(carried, element):
            pair, flag = element
            used = jnp.where(flag, jnp.zeros_like(carried), carried)
            return (used + pair, used)
        _, states = lax.scan(forward_step, jnp.zeros((H, DH, DH), jnp.float32), (key_value, flags))
        state_b = round_keep(states)
        scores = round_keep(jnp.einsum('cthd,cshd->chts', query_feat, key_feat) * causal)
        attn = jnp.einsum('chts,cshe->cthe', scores, value_four) + jnp.einsum('cthd,chde->cthe', query_feat, state_b)
        rms = jnp.sqrt(lax.optimization_barrier(jnp.mean(attn * attn, axis=-1, keepdims=True)) + epsilon)
        normed = attn / rms
        gain_part = lax.optimization_barrier(jnp.sum(normed * cot_four, axis=(0, 1))).reshape(H * DH)
        scaled = gain_heads * cot_four
        center = lax.optimization_barrier(jnp.mean(normed * scaled, axis=-1, keepdims=True))
        attn_grad = round_keep((scaled - normed * center) / rms)
        query_state = jnp.einsum('cthd,cthe->chde', query_feat, attn_grad)

        def backward_step(carried, element):
            pair, flag = element
            following = jnp.where(flag, jnp.zeros_like(carried), carried + pair)
            return (following, carried)
        _, back = lax.scan(backward_step, jnp.zeros((H, DH, DH), jnp.float32), (query_state, flags), reverse=True)
        back_b = round_keep(back)
        mixed = round_keep(jnp.einsum('cthe,cshe->chts', attn_grad, value_four) * causal)
        query_part = jnp.einsum('chts,cshd->cthd', mixed, key_feat) + jnp.einsum('cthe,chde->cthd', attn_grad, state_b)
        key_part = jnp.einsum('chts,cthd->cshd', mixed, query_feat) + jnp.einsum('cshe,chde->cshd', value_four, back_b)
        value_part = jnp.einsum('chts,cthe->cshe', scores, attn_grad) + jnp.einsum('cshd,chde->cshe', key_feat, back_b)
        query_out = (query_part.reshape(length, H * DH) * feature_slope(query_seq)).astype(jnp.bfloat16)
        key_out = (key_part.reshape(length, H * DH) * feature_slope(key_seq)).astype(jnp.bfloat16)
        value_out = value_part.reshape(length, H * DH).astype(jnp.bfloat16)
        return (query_out, key_out, value_out, gain_part)
    query_grad, key_grad, value_grad, gain_parts = lax.map(one_sequence, (queries, key_rows, value_rows, out_cotangent, doc_starts))
    gain_grad = lax.optimization_barrier(jnp.sum(gain_parts, axis=0)) / jnp.sqrt(jnp.float32(SEQS * LEN))
    return (query_grad, key_grad, value_grad, gain_grad)
```

```python
import functools

import jax
import jax.numpy as jnp
from jax import lax
from jax.experimental import pallas as pl
from jax.experimental.pallas import tpu as pltpu
from jax.sharding import PartitionSpec as P

H = 16
DH = 128
SPAN = 128
HALF = H // 2
WIDE = HALF * DH
EPS = 1e-06

F32 = jnp.float32
BF16 = jnp.bfloat16


def dot(a, b, ca, cb):
    return lax.dot_general(a, b, (((ca,), (cb,)), ((), ())), preferred_element_type=F32)


def phi(x):
    wide = x.astype(F32)
    return jnp.where(wide > 0, wide + 1.0, jnp.exp(jnp.minimum(wide, 0.0)))


def slope(x):
    wide = x.astype(F32)
    return jnp.where(wide > 0, 1.0, jnp.exp(jnp.minimum(wide, 0.0)))


def causal():
    rows = lax.broadcasted_iota(jnp.int32, (SPAN, SPAN), 0)
    cols = lax.broadcasted_iota(jnp.int32, (SPAN, SPAN), 1)
    return cols <= rows


def unflagged(starts_ref, block):
    hit = starts_ref[0, 0] == block
    for d in range(1, starts_ref.shape[1]):
        hit = jnp.logical_or(hit, starts_ref[0, d] == block)
    return jnp.where(hit, 0.0, 1.0).astype(F32)


def place():
    c = lax.axis_index("ctx")
    j = lax.rem(c, 2)
    return j, c - j


def columns(j, h):
    return pl.ds(pl.multiple_of(j * WIDE + h * DH, DH), DH)


def head(h):
    return slice(h * DH, (h + 1) * DH)


def pack_kernel(a_ref, b_ref, c_ref, d_ref, ab_ref, cd_ref):
    j, _ = place()
    for h in range(HALF):
        cols = columns(1 - j, h)
        ab_ref[0, :, head(h)] = a_ref[:, cols].astype(F32)
        ab_ref[1, :, head(h)] = b_ref[:, cols].astype(F32)
        cd_ref[0, :, head(h)] = c_ref[:, cols].astype(F32)
        cd_ref[1, :, head(h)] = d_ref[:, cols].astype(F32)


def state_kernel(starts_ref, k_ref, v_ref, got_ref, kk_ref, fk_ref, vv_ref, sent_ref, first_ref):
    j, z = place()
    inner = unflagged(starts_ref, z + 1)
    for h in range(HALF):
        cols = columns(j, h)
        own_k, own_v = k_ref[:, cols], v_ref[:, cols]
        other_k, other_v = got_ref[0, :, head(h)].astype(BF16), got_ref[1, :, head(h)].astype(BF16)
        own_f, other_f = phi(own_k).astype(BF16), phi(other_k).astype(BF16)
        for ref, own, other in ((kk_ref, own_k, other_k), (fk_ref, own_f, other_f), (vv_ref, own_v, other_v)):
            ref[j, :, head(h)] = own
            ref[1 - j, :, head(h)] = other
        own_s, other_s = dot(own_f, own_v, 0, 0), dot(other_f, other_v, 0, 0)
        swap = j == 1
        first = jnp.where(swap, other_s, own_s) * inner
        second = jnp.where(swap, own_s, other_s)
        first_ref[h] = first
        sent_ref[h] = second + first


def local_kernel(q_ref, c_ref, got_ref, fk_ref, vv_ref, qq_ref, fq_ref, cc_ref, scores_ref, attn_ref):
    j, _ = place()
    keep = causal()
    for h in range(HALF):
        cols = columns(j, h)
        own_q, other_q = q_ref[:, cols], got_ref[0, :, head(h)].astype(BF16)
        qq_ref[j, :, head(h)] = own_q
        qq_ref[1 - j, :, head(h)] = other_q
        fq_ref[j, :, head(h)] = phi(own_q).astype(BF16)
        fq_ref[1 - j, :, head(h)] = phi(other_q).astype(BF16)
        cc_ref[j, :, head(h)] = c_ref[:, cols]
        cc_ref[1 - j, :, head(h)] = got_ref[1, :, head(h)].astype(BF16)
    for h in range(HALF):
        for b in range(2):
            raw = dot(fq_ref[b, :, head(h)], fk_ref[b, :, head(h)], 1, 1)
            scores = jnp.where(keep, raw, 0.0).astype(BF16)
            scores_ref[b, h] = scores
            attn_ref[b, :, head(h)] = dot(scores, vv_ref[b, :, head(h)], 1, 0)


def weighted(parts, weights, h):
    total = parts[0][h]
    for part, weight in zip(parts[1:], weights):
        total = total + weight * part[h]
    return total


def link_weights(starts_ref, count, nearest, step):
    weights, block, weight = [], nearest, 1.0
    for _ in range(count - 1):
        weight = weight * unflagged(starts_ref, block) * unflagged(starts_ref, block + step)
        weights.append(weight)
        block = block + 2 * step
    return weights


def norm_kernel(count, starts_ref, gain_ref, *refs):
    parts, refs = refs[:count], refs[count:]
    first_ref, fq_ref, cc_ref, attn_ref, state_ref, ag_ref, sent_ref, second_ref, part_ref = refs
    j, z = place()
    outer, inner = unflagged(starts_ref, z), unflagged(starts_ref, z + 1)
    weights = link_weights(starts_ref, count, z - 1, -1)
    for h in range(HALF):
        entering = outer * weighted(parts, weights, h)
        gain = gain_ref[:, columns(j, h)]
        states = (entering.astype(BF16), (inner * entering + first_ref[h]).astype(BF16))
        partial = jnp.zeros((1, DH), F32)
        grads = []
        for b in range(2):
            state_ref[b, h] = states[b]
            fq = fq_ref[b, :, head(h)]
            attn = attn_ref[b, :, head(h)] + dot(fq, states[b], 1, 0)
            inverse = 1.0 / jnp.sqrt(jnp.mean(attn * attn, axis=-1, keepdims=True) + EPS)
            normed = attn * inverse
            cot = cc_ref[b, :, head(h)].astype(F32)
            partial = partial + jnp.sum(normed * cot, axis=0, keepdims=True)
            scaled = gain * cot
            center = jnp.mean(normed * scaled, axis=-1, keepdims=True)
            ag = ((scaled - normed * center) * inverse).astype(BF16)
            ag_ref[b, :, head(h)] = ag
            grads.append(dot(fq, ag, 0, 0))
        second = inner * grads[1]
        second_ref[h] = second
        sent_ref[h] = grads[0] + second
        part_ref[h : h + 1, :] = partial


def mixed_kernel(ag_ref, vv_ref, fk_ref, fq_ref, qq_ref, scores_ref, state_ref, own_ref, other_ref, kl_ref, vl_ref, qg_ref):
    j, _ = place()
    keep = causal()
    for h in range(HALF):
        for b in range(2):
            ag = ag_ref[b, :, head(h)]
            raw = dot(ag, vv_ref[b, :, head(h)], 1, 1)
            mixed = jnp.where(keep, raw, 0.0).astype(BF16)
            part = dot(mixed, fk_ref[b, :, head(h)], 1, 0) + dot(ag, state_ref[b, h], 1, 1)
            qg_ref[b, :, head(h)] = part * slope(qq_ref[b, :, head(h)])
            kl_ref[b, :, head(h)] = dot(mixed, fq_ref[b, :, head(h)], 0, 0)
            vl_ref[b, :, head(h)] = dot(scores_ref[b, h], ag, 0, 0)
    own_ref[...] = qg_ref[j].astype(BF16)
    other_ref[...] = qg_ref[1 - j]


def final_kernel(count, starts_ref, *refs):
    parts, refs = refs[:count], refs[count:]
    second_ref, kl_ref, vl_ref, vv_ref, fk_ref, kk_ref, own_ref, other_ref, kg_ref, vg_ref = refs
    j, z = place()
    outer, inner = unflagged(starts_ref, z + 2), unflagged(starts_ref, z + 1)
    weights = link_weights(starts_ref, count, z + 3, 1)
    for h in range(HALF):
        entering = outer * weighted(parts, weights, h)
        backs = ((inner * entering + second_ref[h]).astype(BF16), entering.astype(BF16))
        for b in range(2):
            key = kl_ref[b, :, head(h)] + dot(vv_ref[b, :, head(h)], backs[b], 1, 1)
            kg_ref[b, :, head(h)] = key * slope(kk_ref[b, :, head(h)])
            vg_ref[b, :, head(h)] = vl_ref[b, :, head(h)] + dot(fk_ref[b, :, head(h)], backs[b], 1, 0)
    own_ref[0] = kg_ref[j].astype(BF16)
    own_ref[1] = vg_ref[j].astype(BF16)
    other_ref[0] = kg_ref[1 - j]
    other_ref[1] = vg_ref[1 - j]


def join_kernel(q_own_ref, q_got_ref, kv_own_ref, kv_got_ref, q_ref, k_ref, v_ref):
    j, _ = place()
    for h in range(HALF):
        for ref, own, got in (
            (q_ref, q_own_ref, q_got_ref),
            (k_ref, kv_own_ref.at[0], kv_got_ref.at[0]),
            (v_ref, kv_own_ref.at[1], kv_got_ref.at[1]),
        ):
            ref[:, columns(j, h)] = own[:, head(h)]
            ref[:, columns(1 - j, h)] = got[:, head(h)].astype(BF16)


VM = pl.BlockSpec(memory_space=pltpu.VMEM)
SM = pl.BlockSpec(memory_space=pltpu.SMEM)


def call(kernel, name, outs, args, scalars=0, scratch=(), flops=0):
    moved = sum(a.size * a.dtype.itemsize for a in args) + sum(
        o[0][0] * functools.reduce(lambda x, y: x * y, o[0][1:], 1) * jnp.dtype(o[1]).itemsize for o in outs
    )
    return pl.pallas_call(
        kernel,
        out_shape=[jax.ShapeDtypeStruct(s, d) for s, d in outs],
        in_specs=[SM] * scalars + [VM] * (len(args) - scalars),
        out_specs=[VM] * len(outs),
        scratch_shapes=scratch,
        cost_estimate=pl.CostEstimate(flops=flops, bytes_accessed=moved, transcendentals=0),
        name=name,
    )(*args)


def per_device(queries, key_rows, value_rows, out_cotangent, norm_gain, doc_starts):
    count = lax.axis_size("ctx")
    chips = count // 2
    documents = doc_starts.shape[1]
    swap = [(i, i ^ 1) for i in range(count)]
    reach = min(chips - 1, -(-(count - documents) // 2))
    q, k, v, cot = queries[0], key_rows[0], value_rows[0], out_cotangent[0]
    gain = norm_gain.reshape(1, H * DH)
    mm = 2 * HALF * 2 * SPAN * DH * DH

    def hop(x, distance):
        pairs = [
            (2 * i + j, 2 * (i + distance) + j)
            for i in range(chips)
            for j in range(2)
            if 0 <= i + distance < chips
        ]
        return lax.ppermute(x, "ctx", pairs)

    def arriving(x, sign):
        if reach <= 3:
            parts = []
            for _ in range(reach):
                x = hop(x, sign)
                parts.append(x)
            return parts
        starts = doc_starts[0]
        chip = lax.axis_index("ctx") // 2

        def linked(low, high):
            return 1.0 - jnp.any((starts >= low) & (starts <= high)).astype(F32)

        distance = 1
        while distance < chips:
            if sign > 0:
                weight = linked(2 * (chip - distance) + 2, 2 * chip + 1)
            else:
                weight = linked(2 * chip + 1, 2 * (chip + distance))
            x = x + weight * hop(x, sign * distance)
            distance *= 2
        return [hop(x, sign)]

    kv_send, qc_send = call(
        pack_kernel, "pack", [((2, SPAN, WIDE), F32)] * 2, [k, v, q, cot]
    )
    kv_got = lax.ppermute(kv_send, "ctx", swap)
    qc_got = lax.ppermute(qc_send, "ctx", swap)
    rows = ((2, SPAN, WIDE), BF16)
    wide_rows = ((2, SPAN, WIDE), F32)
    square = ((HALF, DH, DH), F32)
    pair_square = ((2, HALF, DH, DH), BF16)
    kk, fk, vv, sent, first = call(
        state_kernel, "state", [rows, rows, rows, square, square], [doc_starts, k, v, kv_got], scalars=1, flops=mm
    )
    parts = arriving(sent, 1)
    qq, fq, cc, scores, attn = call(
        local_kernel, "local", [rows, rows, rows, pair_square, wide_rows], [q, cot, qc_got, fk, vv], flops=2 * mm
    )
    states, ag, sent_back, second, gain_part = call(
        functools.partial(norm_kernel, len(parts)),
        "norm",
        [pair_square, rows, square, square, ((HALF, DH), F32)],
        [doc_starts, gain, *parts, first, fq, cc, attn],
        scalars=1,
        flops=2 * mm,
    )
    parts_back = arriving(sent_back, -1)
    q_own, q_send, k_local, v_local = call(
        mixed_kernel,
        "mixed",
        [((SPAN, WIDE), BF16), ((SPAN, WIDE), F32), wide_rows, wide_rows],
        [ag, vv, fk, fq, qq, scores, states],
        scratch=[pltpu.VMEM((2, SPAN, WIDE), F32)],
        flops=5 * mm,
    )
    q_got = lax.ppermute(q_send, "ctx", swap)
    total = gain_part
    for axis, size in (("dp", lax.axis_size("dp")), ("ctx", count)):
        bit = 1 if axis == "dp" else 2
        while bit < size:
            total = total + lax.ppermute(total, axis, [(i, i ^ bit) for i in range(size)])
            bit *= 2
    total_other = lax.ppermute(total, "ctx", swap)
    kv_own, kv_back = call(
        functools.partial(final_kernel, len(parts_back)),
        "final",
        [((2, SPAN, WIDE), BF16), ((2, SPAN, WIDE), F32)],
        [doc_starts, *parts_back, second, k_local, v_local, vv, fk, kk],
        scalars=1,
        scratch=[pltpu.VMEM((2, SPAN, WIDE), F32)] * 2,
        flops=2 * mm,
    )
    kv_back_got = lax.ppermute(kv_back, "ctx", swap)
    full = ((SPAN, H * DH), BF16)
    query_grad, key_grad, value_grad = call(
        join_kernel, "join", [full] * 3, [q_own, q_got, kv_own, kv_back_got]
    )
    own_first = lax.axis_index("ctx") % 2 == 0
    low = jnp.where(own_first, total, total_other)
    high = jnp.where(own_first, total_other, total)
    gain_grad = jnp.concatenate([low, high]).reshape(H * DH) / jnp.sqrt(
        jnp.float32(lax.axis_size("dp") * SPAN * count)
    )
    return query_grad[None], key_grad[None], value_grad[None], gain_grad


def solution(mesh):
    placed = (
        P("dp", "ctx", None),
        P("dp", "ctx", None),
        P("dp", "ctx", None),
        P("dp", "ctx", None),
        P(),
        P("dp", None),
    )
    return jax.shard_map(
        per_device,
        mesh=mesh,
        in_specs=placed,
        out_specs=(P("dp", "ctx", None), P("dp", "ctx", None), P("dp", "ctx", None), P()),
        check_vma=False,
    )
```

```python
import functools

import jax
import jax.numpy as jnp
from jax import lax
from jax.experimental import pallas as pl
from jax.experimental.pallas import tpu as pltpu
from jax.sharding import PartitionSpec as P

H = 16
DH = 128
SPAN = 128
HALF = H // 2
WIDE = HALF * DH
EPS = 1e-06

F32 = jnp.float32
BF16 = jnp.bfloat16


def dot(a, b, ca, cb):
    return lax.dot_general(a, b, (((ca,), (cb,)), ((), ())), preferred_element_type=F32)


def phi(x):
    wide = x.astype(F32)
    return jnp.where(wide > 0, wide + 1.0, jnp.exp(jnp.minimum(wide, 0.0)))


def slope(x):
    wide = x.astype(F32)
    return jnp.where(wide > 0, 1.0, jnp.exp(jnp.minimum(wide, 0.0)))


def causal():
    rows = lax.broadcasted_iota(jnp.int32, (SPAN, SPAN), 0)
    cols = lax.broadcasted_iota(jnp.int32, (SPAN, SPAN), 1)
    return cols <= rows


def unflagged(starts_ref, block):
    hit = starts_ref[0, 0] == block
    for d in range(1, starts_ref.shape[1]):
        hit = jnp.logical_or(hit, starts_ref[0, d] == block)
    return jnp.where(hit, 0.0, 1.0).astype(F32)


def place():
    c = lax.axis_index("ctx")
    j = lax.rem(c, 2)
    return j, c - j


def columns(j, h):
    return pl.ds(pl.multiple_of(j * WIDE + h * DH, DH), DH)


def head(h):
    return slice(h * DH, (h + 1) * DH)


def pack_kernel(a_ref, b_ref, c_ref, d_ref, ab_ref, cd_ref):
    j, _ = place()
    for h in range(HALF):
        cols = columns(1 - j, h)
        ab_ref[0, :, head(h)] = a_ref[:, cols].astype(F32)
        ab_ref[1, :, head(h)] = b_ref[:, cols].astype(F32)
        cd_ref[0, :, head(h)] = c_ref[:, cols].astype(F32)
        cd_ref[1, :, head(h)] = d_ref[:, cols].astype(F32)


def state_kernel(starts_ref, k_ref, v_ref, got_ref, kk_ref, fk_ref, vv_ref, sent_ref, first_ref):
    j, z = place()
    inner = unflagged(starts_ref, z + 1)
    for h in range(HALF):
        cols = columns(j, h)
        own_k, own_v = k_ref[:, cols], v_ref[:, cols]
        other_k, other_v = got_ref[0, :, head(h)].astype(BF16), got_ref[1, :, head(h)].astype(BF16)
        own_f, other_f = phi(own_k).astype(BF16), phi(other_k).astype(BF16)
        for ref, own, other in ((kk_ref, own_k, other_k), (fk_ref, own_f, other_f), (vv_ref, own_v, other_v)):
            ref[j, :, head(h)] = own
            ref[1 - j, :, head(h)] = other
        own_s, other_s = dot(own_f, own_v, 0, 0), dot(other_f, other_v, 0, 0)
        swap = j == 1
        first = jnp.where(swap, other_s, own_s) * inner
        second = jnp.where(swap, own_s, other_s)
        first_ref[h] = first
        sent_ref[h] = second + first


def local_kernel(q_ref, c_ref, got_ref, fk_ref, vv_ref, qq_ref, fq_ref, cc_ref, scores_ref, attn_ref):
    j, _ = place()
    keep = causal()
    for h in range(HALF):
        cols = columns(j, h)
        own_q, other_q = q_ref[:, cols], got_ref[0, :, head(h)].astype(BF16)
        qq_ref[j, :, head(h)] = own_q
        qq_ref[1 - j, :, head(h)] = other_q
        fq_ref[j, :, head(h)] = phi(own_q).astype(BF16)
        fq_ref[1 - j, :, head(h)] = phi(other_q).astype(BF16)
        cc_ref[j, :, head(h)] = c_ref[:, cols]
        cc_ref[1 - j, :, head(h)] = got_ref[1, :, head(h)].astype(BF16)
    for h in range(HALF):
        for b in range(2):
            raw = dot(fq_ref[b, :, head(h)], fk_ref[b, :, head(h)], 1, 1)
            scores = jnp.where(keep, raw, 0.0).astype(BF16)
            scores_ref[b, h] = scores
            attn_ref[b, :, head(h)] = dot(scores, vv_ref[b, :, head(h)], 1, 0)


def weighted(parts, weights, h):
    total = parts[0][h]
    for part, weight in zip(parts[1:], weights):
        total = total + weight * part[h]
    return total


def link_weights(starts_ref, count, nearest, step):
    weights, block, weight = [], nearest, 1.0
    for _ in range(count - 1):
        weight = weight * unflagged(starts_ref, block) * unflagged(starts_ref, block + step)
        weights.append(weight)
        block = block + 2 * step
    return weights


def norm_kernel(count, starts_ref, gain_ref, *refs):
    parts, refs = refs[:count], refs[count:]
    first_ref, fq_ref, cc_ref, attn_ref, state_ref, ag_ref, sent_ref, second_ref, part_ref = refs
    j, z = place()
    outer, inner = unflagged(starts_ref, z), unflagged(starts_ref, z + 1)
    weights = link_weights(starts_ref, count, z - 1, -1)
    for h in range(HALF):
        entering = outer * weighted(parts, weights, h)
        gain = gain_ref[:, columns(j, h)]
        states = (entering.astype(BF16), (inner * entering + first_ref[h]).astype(BF16))
        partial = jnp.zeros((1, DH), F32)
        grads = []
        for b in range(2):
            state_ref[b, h] = states[b]
            fq = fq_ref[b, :, head(h)]
            attn = attn_ref[b, :, head(h)] + dot(fq, states[b], 1, 0)
            inverse = 1.0 / jnp.sqrt(jnp.mean(attn * attn, axis=-1, keepdims=True) + EPS)
            normed = attn * inverse
            cot = cc_ref[b, :, head(h)].astype(F32)
            partial = partial + jnp.sum(normed * cot, axis=0, keepdims=True)
            scaled = gain * cot
            center = jnp.mean(normed * scaled, axis=-1, keepdims=True)
            ag = ((scaled - normed * center) * inverse).astype(BF16)
            ag_ref[b, :, head(h)] = ag
            grads.append(dot(fq, ag, 0, 0))
        second = inner * grads[1]
        second_ref[h] = second
        sent_ref[h] = grads[0] + second
        part_ref[h : h + 1, :] = partial


def mixed_kernel(ag_ref, vv_ref, fk_ref, fq_ref, qq_ref, scores_ref, state_ref, own_ref, other_ref, kl_ref, vl_ref, qg_ref):
    j, _ = place()
    keep = causal()
    for h in range(HALF):
        for b in range(2):
            ag = ag_ref[b, :, head(h)]
            raw = dot(ag, vv_ref[b, :, head(h)], 1, 1)
            mixed = jnp.where(keep, raw, 0.0).astype(BF16)
            part = dot(mixed, fk_ref[b, :, head(h)], 1, 0) + dot(ag, state_ref[b, h], 1, 1)
            qg_ref[b, :, head(h)] = part * slope(qq_ref[b, :, head(h)])
            kl_ref[b, :, head(h)] = dot(mixed, fq_ref[b, :, head(h)], 0, 0)
            vl_ref[b, :, head(h)] = dot(scores_ref[b, h], ag, 0, 0)
    own_ref[...] = qg_ref[j].astype(BF16)
    other_ref[...] = qg_ref[1 - j]


def final_kernel(count, starts_ref, *refs):
    parts, refs = refs[:count], refs[count:]
    second_ref, kl_ref, vl_ref, vv_ref, fk_ref, kk_ref, own_ref, other_ref, kg_ref, vg_ref = refs
    j, z = place()
    outer, inner = unflagged(starts_ref, z + 2), unflagged(starts_ref, z + 1)
    weights = link_weights(starts_ref, count, z + 3, 1)
    for h in range(HALF):
        entering = outer * weighted(parts, weights, h)
        backs = ((inner * entering + second_ref[h]).astype(BF16), entering.astype(BF16))
        for b in range(2):
            key = kl_ref[b, :, head(h)] + dot(vv_ref[b, :, head(h)], backs[b], 1, 1)
            kg_ref[b, :, head(h)] = key * slope(kk_ref[b, :, head(h)])
            vg_ref[b, :, head(h)] = vl_ref[b, :, head(h)] + dot(fk_ref[b, :, head(h)], backs[b], 1, 0)
    own_ref[0] = kg_ref[j].astype(BF16)
    own_ref[1] = vg_ref[j].astype(BF16)
    other_ref[0] = kg_ref[1 - j]
    other_ref[1] = vg_ref[1 - j]


def join_kernel(tokens, q_own_ref, q_got_ref, kv_own_ref, kv_got_ref, total_ref, total_got_ref, q_ref, k_ref, v_ref, gain_ref):
    j, _ = place()
    root = jnp.sqrt(F32(tokens))
    gain_ref[pl.ds(pl.multiple_of(j * HALF, HALF), HALF), :] = total_ref[...] / root
    gain_ref[pl.ds(pl.multiple_of((1 - j) * HALF, HALF), HALF), :] = total_got_ref[...] / root
    for h in range(HALF):
        for ref, own, got in (
            (q_ref, q_own_ref, q_got_ref),
            (k_ref, kv_own_ref.at[0], kv_got_ref.at[0]),
            (v_ref, kv_own_ref.at[1], kv_got_ref.at[1]),
        ):
            ref[:, columns(j, h)] = own[:, head(h)]
            ref[:, columns(1 - j, h)] = got[:, head(h)].astype(BF16)


VM = pl.BlockSpec(memory_space=pltpu.VMEM)
SM = pl.BlockSpec(memory_space=pltpu.SMEM)


def call(kernel, name, outs, args, scalars=0, scratch=(), flops=0):
    moved = sum(a.size * a.dtype.itemsize for a in args) + sum(
        o[0][0] * functools.reduce(lambda x, y: x * y, o[0][1:], 1) * jnp.dtype(o[1]).itemsize for o in outs
    )
    return pl.pallas_call(
        kernel,
        out_shape=[jax.ShapeDtypeStruct(s, d) for s, d in outs],
        in_specs=[SM] * scalars + [VM] * (len(args) - scalars),
        out_specs=[VM] * len(outs),
        scratch_shapes=scratch,
        compiler_params=pltpu.CompilerParams(vmem_limit_bytes=24 * 1024 * 1024),
        cost_estimate=pl.CostEstimate(flops=flops, bytes_accessed=moved, transcendentals=0),
        name=name,
    )(*args)


def per_device(queries, key_rows, value_rows, out_cotangent, norm_gain, doc_starts):
    count = lax.axis_size("ctx")
    chips = count // 2
    documents = doc_starts.shape[1]
    swap = [(i, i ^ 1) for i in range(count)]
    reach = min(chips - 1, -(-(count - documents) // 2))
    q, k, v, cot = queries[0], key_rows[0], value_rows[0], out_cotangent[0]
    gain = norm_gain.reshape(1, H * DH)
    mm = 2 * HALF * 2 * SPAN * DH * DH

    def hop(x, distance):
        pairs = [
            (2 * i + j, 2 * (i + distance) + j)
            for i in range(chips)
            for j in range(2)
            if 0 <= i + distance < chips
        ]
        return lax.ppermute(x, "ctx", pairs)

    def arriving(x, sign, beside):
        if reach <= 3:
            parts = []
            for _ in range(reach):
                x = hop(x, sign)
                if not parts and beside is not None:
                    x, beside = lax.optimization_barrier((x, beside))
                parts.append(x)
            return parts, beside
        starts = doc_starts[0]
        chip = lax.axis_index("ctx") // 2

        def linked(low, high):
            return 1.0 - jnp.any((starts >= low) & (starts <= high)).astype(F32)

        distance = 1
        while distance < chips:
            if sign > 0:
                weight = linked(2 * (chip - distance) + 2, 2 * chip + 1)
            else:
                weight = linked(2 * chip + 1, 2 * (chip + distance))
            x = x + weight * hop(x, sign * distance)
            distance *= 2
        return [hop(x, sign)], beside

    kv_send, qc_send = call(
        pack_kernel, "pack", [((2, SPAN, WIDE), F32)] * 2, [k, v, q, cot]
    )
    kv_got = lax.ppermute(kv_send, "ctx", swap)
    qc_got = lax.ppermute(qc_send, "ctx", swap)
    rows = ((2, SPAN, WIDE), BF16)
    wide_rows = ((2, SPAN, WIDE), F32)
    square = ((HALF, DH, DH), F32)
    pair_square = ((2, HALF, DH, DH), BF16)
    kk, fk, vv, sent, first = call(
        state_kernel, "state", [rows, rows, rows, square, square], [doc_starts, k, v, kv_got], scalars=1, flops=mm
    )
    parts, _ = arriving(sent, 1, None)
    qq, fq, cc, scores, attn = call(
        local_kernel, "local", [rows, rows, rows, pair_square, wide_rows], [q, cot, qc_got, fk, vv], flops=2 * mm
    )
    states, ag, sent_back, second, gain_part = call(
        functools.partial(norm_kernel, len(parts)),
        "norm",
        [pair_square, rows, square, square, ((HALF, DH), F32)],
        [doc_starts, gain, *parts, first, fq, cc, attn],
        scalars=1,
        flops=2 * mm,
    )
    total = gain_part
    steps = []
    for axis, size in (("dp", lax.axis_size("dp")), ("ctx", count)):
        bit = 1 if axis == "dp" else 2
        while bit < size:
            steps.append((axis, [(i, i ^ bit) for i in range(size)]))
            bit *= 2
    for axis, pairs in steps[:-1]:
        total = total + lax.ppermute(total, axis, pairs)
    parts_back, total = arriving(sent_back, -1, total)
    q_own, q_send, k_local, v_local = call(
        mixed_kernel,
        "mixed",
        [((SPAN, WIDE), BF16), ((SPAN, WIDE), F32), wide_rows, wide_rows],
        [ag, vv, fk, fq, qq, scores, states],
        scratch=[pltpu.VMEM((2, SPAN, WIDE), F32)],
        flops=5 * mm,
    )
    q_got = lax.ppermute(q_send, "ctx", swap)
    for axis, pairs in steps[-1:]:
        total = total + lax.ppermute(total, axis, pairs)
    second, total = lax.optimization_barrier((second, total))
    total_other = lax.ppermute(total, "ctx", swap)
    kv_own, kv_back = call(
        functools.partial(final_kernel, len(parts_back)),
        "final",
        [((2, SPAN, WIDE), BF16), ((2, SPAN, WIDE), F32)],
        [doc_starts, *parts_back, second, k_local, v_local, vv, fk, kk],
        scalars=1,
        scratch=[pltpu.VMEM((2, SPAN, WIDE), F32)] * 2,
        flops=2 * mm,
    )
    kv_back_got = lax.ppermute(kv_back, "ctx", swap)
    full = ((SPAN, H * DH), BF16)
    query_grad, key_grad, value_grad, gain_grad = call(
        functools.partial(join_kernel, lax.axis_size("dp") * SPAN * count),
        "join",
        [full] * 3 + [((H, DH), F32)],
        [q_own, q_got, kv_own, kv_back_got, total, total_other],
    )
    return query_grad[None], key_grad[None], value_grad[None], gain_grad.reshape(H * DH)


def solution(mesh):
    placed = (
        P("dp", "ctx", None),
        P("dp", "ctx", None),
        P("dp", "ctx", None),
        P("dp", "ctx", None),
        P(),
        P("dp", None),
    )
    return jax.shard_map(
        per_device,
        mesh=mesh,
        in_specs=placed,
        out_specs=(P("dp", "ctx", None), P("dp", "ctx", None), P("dp", "ctx", None), P()),
        check_vma=False,
    )
```

```python
import functools

import jax
import jax.numpy as jnp
from jax import lax
from jax.experimental import pallas as pl
from jax.experimental.pallas import tpu as pltpu
from jax.sharding import PartitionSpec as P

H = 16
DH = 128
SPAN = 128
HALF = H // 2
WIDE = HALF * DH
EPS = 1e-06
LAG = 5000

F32 = jnp.float32
BF16 = jnp.bfloat16


def dot(a, b, ca, cb):
    return lax.dot_general(a, b, (((ca,), (cb,)), ((), ())), preferred_element_type=F32)


def phi(x):
    wide = x.astype(F32)
    return jnp.where(wide > 0, wide + 1.0, jnp.exp(jnp.minimum(wide, 0.0)))


def slope(x):
    wide = x.astype(F32)
    return jnp.where(wide > 0, 1.0, jnp.exp(jnp.minimum(wide, 0.0)))


def causal():
    rows = lax.broadcasted_iota(jnp.int32, (SPAN, SPAN), 0)
    cols = lax.broadcasted_iota(jnp.int32, (SPAN, SPAN), 1)
    return cols <= rows


def unflagged(starts_ref, block):
    hit = starts_ref[0, 0] == block
    for d in range(1, starts_ref.shape[1]):
        hit = jnp.logical_or(hit, starts_ref[0, d] == block)
    return jnp.where(hit, 0.0, 1.0).astype(F32)


def place():
    c = lax.axis_index("ctx")
    j = lax.rem(c, 2)
    return j, c - j


def columns(j, h):
    return pl.ds(pl.multiple_of(j * WIDE + h * DH, DH), DH)


def head(h):
    return slice(h * DH, (h + 1) * DH)


def pack_kernel(a_ref, b_ref, c_ref, d_ref, ab_ref, cd_ref, held, sems):
    j, _ = place()
    half = pl.ds(pl.multiple_of((1 - j) * WIDE, WIDE), WIDE)
    copies = [
        pltpu.make_async_copy(ref.at[:, half], held.at[i], sems.at[i])
        for i, ref in enumerate((a_ref, b_ref, c_ref, d_ref))
    ]
    for copy in copies:
        copy.start()
    for i, copy in enumerate(copies):
        copy.wait()
        (ab_ref if i < 2 else cd_ref)[i % 2] = held[i].astype(F32)


def state_kernel(starts_ref, k_ref, v_ref, got_ref, kk_ref, fk_ref, vv_ref, sent_ref, first_ref):
    j, z = place()
    inner = unflagged(starts_ref, z + 1)
    for h in range(HALF):
        cols = columns(j, h)
        own_k, own_v = k_ref[:, cols], v_ref[:, cols]
        other_k, other_v = got_ref[0, :, head(h)].astype(BF16), got_ref[1, :, head(h)].astype(BF16)
        own_f, other_f = phi(own_k).astype(BF16), phi(other_k).astype(BF16)
        for ref, own, other in ((kk_ref, own_k, other_k), (fk_ref, own_f, other_f), (vv_ref, own_v, other_v)):
            ref[j, :, head(h)] = own
            ref[1 - j, :, head(h)] = other
        own_s, other_s = dot(own_f, own_v, 0, 0), dot(other_f, other_v, 0, 0)
        swap = j == 1
        first = jnp.where(swap, other_s, own_s) * inner
        second = jnp.where(swap, own_s, other_s)
        first_ref[h] = first
        sent_ref[h] = second + first


def local_kernel(turn, lag, *refs):
    j, _ = place()

    @pl.when(j == turn)
    def _():
        local_part(j, *refs[:5], *refs[-5:])
        if lag:
            pl.delay(lag)


def local_part(j, q_ref, c_ref, got_ref, fk_ref, vv_ref, qq_ref, fq_ref, cc_ref, scores_ref, attn_ref):
    keep = causal()
    for h in range(HALF):
        cols = columns(j, h)
        own_q, other_q = q_ref[:, cols], got_ref[0, :, head(h)].astype(BF16)
        qq_ref[j, :, head(h)] = own_q
        qq_ref[1 - j, :, head(h)] = other_q
        fq_ref[j, :, head(h)] = phi(own_q).astype(BF16)
        fq_ref[1 - j, :, head(h)] = phi(other_q).astype(BF16)
        cc_ref[j, :, head(h)] = c_ref[:, cols]
        cc_ref[1 - j, :, head(h)] = got_ref[1, :, head(h)].astype(BF16)
    for h in range(HALF):
        for b in range(2):
            raw = dot(fq_ref[b, :, head(h)], fk_ref[b, :, head(h)], 1, 1)
            scores = jnp.where(keep, raw, 0.0).astype(BF16)
            scores_ref[b, h] = scores
            attn_ref[b, :, head(h)] = dot(scores, vv_ref[b, :, head(h)], 1, 0)


def weighted(parts, weights, h):
    total = parts[0][h]
    for part, weight in zip(parts[1:], weights):
        total = total + weight * part[h]
    return total


def link_weights(starts_ref, count, nearest, step):
    weights, block, weight = [], nearest, 1.0
    for _ in range(count - 1):
        weight = weight * unflagged(starts_ref, block) * unflagged(starts_ref, block + step)
        weights.append(weight)
        block = block + 2 * step
    return weights


def norm_kernel(count, starts_ref, gain_ref, *refs):
    parts, refs = refs[:count], refs[count:]
    first_ref, fq_ref, cc_ref, attn_ref, state_ref, ag_ref, sent_ref, second_ref, part_ref = refs
    j, z = place()
    outer, inner = unflagged(starts_ref, z), unflagged(starts_ref, z + 1)
    weights = link_weights(starts_ref, count, z - 1, -1)
    for h in range(HALF):
        entering = outer * weighted(parts, weights, h)
        gain = gain_ref[:, columns(j, h)]
        states = (entering.astype(BF16), (inner * entering + first_ref[h]).astype(BF16))
        partial = jnp.zeros((1, DH), F32)
        grads = []
        for b in range(2):
            state_ref[b, h] = states[b]
            fq = fq_ref[b, :, head(h)]
            attn = attn_ref[b, :, head(h)] + dot(fq, states[b], 1, 0)
            inverse = 1.0 / jnp.sqrt(jnp.mean(attn * attn, axis=-1, keepdims=True) + EPS)
            normed = attn * inverse
            cot = cc_ref[b, :, head(h)].astype(F32)
            partial = partial + jnp.sum(normed * cot, axis=0, keepdims=True)
            scaled = gain * cot
            center = jnp.mean(normed * scaled, axis=-1, keepdims=True)
            ag = ((scaled - normed * center) * inverse).astype(BF16)
            ag_ref[b, :, head(h)] = ag
            grads.append(dot(fq, ag, 0, 0))
        second = inner * grads[1]
        second_ref[h] = second
        sent_ref[h] = grads[0] + second
        part_ref[h : h + 1, :] = partial


def mixed_kernel(ag_ref, vv_ref, fk_ref, fq_ref, qq_ref, scores_ref, state_ref, own_ref, other_ref, kl_ref, vl_ref, qg_ref):
    j, _ = place()
    keep = causal()
    for h in range(HALF):
        for b in range(2):
            ag = ag_ref[b, :, head(h)]
            raw = dot(ag, vv_ref[b, :, head(h)], 1, 1)
            mixed = jnp.where(keep, raw, 0.0).astype(BF16)
            part = dot(mixed, fk_ref[b, :, head(h)], 1, 0) + dot(ag, state_ref[b, h], 1, 1)
            qg_ref[b, :, head(h)] = part * slope(qq_ref[b, :, head(h)])
            kl_ref[b, :, head(h)] = dot(mixed, fq_ref[b, :, head(h)], 0, 0)
            vl_ref[b, :, head(h)] = dot(scores_ref[b, h], ag, 0, 0)
    own_ref[...] = qg_ref[j].astype(BF16)
    other_ref[...] = qg_ref[1 - j]


def final_kernel(count, starts_ref, *refs):
    parts, refs = refs[:count], refs[count:]
    second_ref, kl_ref, vl_ref, vv_ref, fk_ref, kk_ref, own_ref, other_ref, kg_ref, vg_ref = refs
    j, z = place()
    outer, inner = unflagged(starts_ref, z + 2), unflagged(starts_ref, z + 1)
    weights = link_weights(starts_ref, count, z + 3, 1)
    for h in range(HALF):
        entering = outer * weighted(parts, weights, h)
        backs = ((inner * entering + second_ref[h]).astype(BF16), entering.astype(BF16))
        for b in range(2):
            key = kl_ref[b, :, head(h)] + dot(vv_ref[b, :, head(h)], backs[b], 1, 1)
            kg_ref[b, :, head(h)] = key * slope(kk_ref[b, :, head(h)])
            vg_ref[b, :, head(h)] = vl_ref[b, :, head(h)] + dot(fk_ref[b, :, head(h)], backs[b], 1, 0)
    own_ref[0] = kg_ref[j].astype(BF16)
    own_ref[1] = vg_ref[j].astype(BF16)
    other_ref[0] = kg_ref[1 - j]
    other_ref[1] = vg_ref[1 - j]


def join_kernel(tokens, q_own_ref, q_got_ref, kv_own_ref, kv_got_ref, total_ref, total_got_ref, q_ref, k_ref, v_ref, gain_ref):
    j, _ = place()
    root = jnp.sqrt(F32(tokens))
    gain_ref[pl.ds(pl.multiple_of(j * HALF, HALF), HALF), :] = total_ref[...] / root
    gain_ref[pl.ds(pl.multiple_of((1 - j) * HALF, HALF), HALF), :] = total_got_ref[...] / root
    for h in range(HALF):
        for ref, own, got in (
            (q_ref, q_own_ref, q_got_ref),
            (k_ref, kv_own_ref.at[0], kv_got_ref.at[0]),
            (v_ref, kv_own_ref.at[1], kv_got_ref.at[1]),
        ):
            ref[:, columns(j, h)] = own[:, head(h)]
            ref[:, columns(1 - j, h)] = got[:, head(h)].astype(BF16)


VM = pl.BlockSpec(memory_space=pltpu.VMEM)
SM = pl.BlockSpec(memory_space=pltpu.SMEM)
HB = pl.BlockSpec(memory_space=pltpu.HBM)


def call(kernel, name, outs, args, scalars=0, whole=(), aliases={}, scratch=(), flops=0):
    moved = sum(a.size * a.dtype.itemsize for a in args) + sum(
        o[0][0] * functools.reduce(lambda x, y: x * y, o[0][1:], 1) * jnp.dtype(o[1]).itemsize for o in outs
    )
    return pl.pallas_call(
        kernel,
        out_shape=[jax.ShapeDtypeStruct(s, d) for s, d in outs],
        in_specs=[SM if i < scalars else HB if i in whole else VM for i in range(len(args))],
        input_output_aliases=aliases,
        out_specs=[VM] * len(outs),
        scratch_shapes=scratch,
        compiler_params=pltpu.CompilerParams(vmem_limit_bytes=24 * 1024 * 1024),
        cost_estimate=pl.CostEstimate(flops=flops, bytes_accessed=moved, transcendentals=0),
        name=name,
    )(*args)


def per_device(queries, key_rows, value_rows, out_cotangent, norm_gain, doc_starts):
    count = lax.axis_size("ctx")
    chips = count // 2
    documents = doc_starts.shape[1]
    swap = [(i, i ^ 1) for i in range(count)]
    reach = min(chips - 1, -(-(count - documents) // 2))
    q, k, v, cot = queries[0], key_rows[0], value_rows[0], out_cotangent[0]
    gain = norm_gain.reshape(1, H * DH)
    mm = 2 * HALF * 2 * SPAN * DH * DH

    def hop(x, distance):
        pairs = [
            (2 * i + j, 2 * (i + distance) + j)
            for i in range(chips)
            for j in range(2)
            if 0 <= i + distance < chips
        ]
        return lax.ppermute(x, "ctx", pairs)

    def arriving(x, sign, beside):
        if reach <= 3:
            parts = []
            for _ in range(reach):
                x = hop(x, sign)
                if not parts and beside is not None:
                    x, beside = lax.optimization_barrier((x, beside))
                parts.append(x)
            return parts, beside
        starts = doc_starts[0]
        chip = lax.axis_index("ctx") // 2

        def linked(low, high):
            return 1.0 - jnp.any((starts >= low) & (starts <= high)).astype(F32)

        distance = 1
        while distance < chips:
            if sign > 0:
                weight = linked(2 * (chip - distance) + 2, 2 * chip + 1)
            else:
                weight = linked(2 * chip + 1, 2 * (chip + distance))
            x = x + weight * hop(x, sign * distance)
            distance *= 2
        return [hop(x, sign)], beside

    kv_send, qc_send = call(
        pack_kernel,
        "pack",
        [((2, SPAN, WIDE), F32)] * 2,
        [pltpu.with_memory_space_constraint(x, pltpu.HBM) for x in (k, v, q, cot)],
        whole=(0, 1, 2, 3),
        scratch=[pltpu.VMEM((4, SPAN, WIDE), BF16), pltpu.SemaphoreType.DMA((4,))],
    )
    kv_got = lax.ppermute(kv_send, "ctx", swap)
    qc_got = lax.ppermute(qc_send, "ctx", swap)
    rows = ((2, SPAN, WIDE), BF16)
    wide_rows = ((2, SPAN, WIDE), F32)
    square = ((HALF, DH, DH), F32)
    pair_square = ((2, HALF, DH, DH), BF16)
    kk, fk, vv, sent, first = call(
        state_kernel, "state", [rows, rows, rows, square, square], [doc_starts, k, v, kv_got], scalars=1, flops=mm
    )
    kinds = [rows, rows, rows, pair_square, wide_rows]
    inputs = [q, cot, qc_got, fk, vv]
    early = call(functools.partial(local_kernel, 1, LAG), "early", kinds, inputs, flops=mm)
    sent, early = lax.optimization_barrier((sent, early))
    late = call(
        functools.partial(local_kernel, 0, 0),
        "late",
        kinds,
        [*inputs, *early],
        aliases={5 + i: i for i in range(5)},
        flops=mm,
    )
    parts, late = arriving(sent, 1, late)
    qq, fq, cc, scores, attn = late
    states, ag, sent_back, second, gain_part = call(
        functools.partial(norm_kernel, len(parts)),
        "norm",
        [pair_square, rows, square, square, ((HALF, DH), F32)],
        [doc_starts, gain, *parts, first, fq, cc, attn],
        scalars=1,
        flops=2 * mm,
    )
    total = gain_part
    dp = lax.axis_size("dp")
    for axis, size, low in (("dp", dp, 1), ("ctx", chips // 2, 2)):
        bit = low
        while bit < size:
            pairs = [(i, i ^ bit) for i in range(lax.axis_size(axis))]
            total = total + lax.ppermute(total, axis, pairs)
            bit *= 2
    far = [lax.axis_size("ctx") // 4, lax.axis_size("ctx") // 2]
    parts_back, total = arriving(sent_back, -1, total)
    q_own, q_send, k_local, v_local = call(
        mixed_kernel,
        "mixed",
        [((SPAN, WIDE), BF16), ((SPAN, WIDE), F32), wide_rows, wide_rows],
        [ag, vv, fk, fq, qq, scores, states],
        scratch=[pltpu.VMEM((2, SPAN, WIDE), F32)],
        flops=5 * mm,
    )
    q_got = lax.ppermute(q_send, "ctx", swap)
    near, side, cross = (
        lax.ppermute(total, "ctx", [(i, i ^ bit) for i in range(count)]) for bit in (far[0], far[1], far[0] + far[1])
    )
    total = (total + near) + (side + cross)
    second, total = lax.optimization_barrier((second, total))
    total_other = lax.ppermute(total, "ctx", swap)
    kv_own, kv_back = call(
        functools.partial(final_kernel, len(parts_back)),
        "final",
        [((2, SPAN, WIDE), BF16), ((2, SPAN, WIDE), F32)],
        [doc_starts, *parts_back, second, k_local, v_local, vv, fk, kk],
        scalars=1,
        scratch=[pltpu.VMEM((2, SPAN, WIDE), F32)] * 2,
        flops=2 * mm,
    )
    kv_back_got = lax.ppermute(kv_back, "ctx", swap)
    full = ((SPAN, H * DH), BF16)
    query_grad, key_grad, value_grad, gain_grad = call(
        functools.partial(join_kernel, dp * SPAN * count),
        "join",
        [full] * 3 + [((H, DH), F32)],
        [q_own, q_got, kv_own, kv_back_got, total, total_other],
    )
    return query_grad[None], key_grad[None], value_grad[None], gain_grad.reshape(H * DH)


def solution(mesh):
    placed = (
        P("dp", "ctx", None),
        P("dp", "ctx", None),
        P("dp", "ctx", None),
        P("dp", "ctx", None),
        P(),
        P("dp", None),
    )
    return jax.shard_map(
        per_device,
        mesh=mesh,
        in_specs=placed,
        out_specs=(P("dp", "ctx", None), P("dp", "ctx", None), P("dp", "ctx", None), P()),
        check_vma=False,
    )
```

```python
import functools

import jax
import jax.numpy as jnp
from jax import lax
from jax.experimental import pallas as pl
from jax.experimental.pallas import tpu as pltpu
from jax.sharding import PartitionSpec as P

H = 16
DH = 128
SPAN = 128
HALF = H // 2
WIDE = HALF * DH
EPS = 1e-06
GROUPS = 2
SIZE = HALF // GROUPS
SLIM = SIZE * DH

F32 = jnp.float32
BF16 = jnp.bfloat16


def dot(a, b, ca, cb):
    return lax.dot_general(a, b, (((ca,), (cb,)), ((), ())), preferred_element_type=F32)


def phi(x):
    wide = x.astype(F32)
    return jnp.where(wide > 0, wide + 1.0, jnp.exp(jnp.minimum(wide, 0.0)))


def slope(x):
    wide = x.astype(F32)
    return jnp.where(wide > 0, 1.0, jnp.exp(jnp.minimum(wide, 0.0)))


def causal():
    rows = lax.broadcasted_iota(jnp.int32, (SPAN, SPAN), 0)
    cols = lax.broadcasted_iota(jnp.int32, (SPAN, SPAN), 1)
    return cols <= rows


def unflagged(starts_ref, block):
    hit = jnp.logical_or(block <= 0, block >= lax.axis_size("ctx"))
    for d in range(starts_ref.shape[1]):
        hit = jnp.logical_or(hit, starts_ref[0, d] == block)
    return jnp.where(hit, 0.0, 1.0).astype(F32)


def place():
    c = lax.axis_index("ctx")
    j = lax.rem(c, 2)
    return j, c - j


def columns(j, h):
    return pl.ds(pl.multiple_of(j * WIDE + h * DH, DH), DH)


def head(h):
    return slice(h * DH, (h + 1) * DH)


def pack_kernel(a_ref, b_ref, c_ref, d_ref, ab_ref, cd_ref, held, sems):
    j, _ = place()
    half = pl.ds(pl.multiple_of((1 - j) * WIDE, WIDE), WIDE)
    copies = [
        pltpu.make_async_copy(ref.at[:, half], held.at[i], sems.at[i])
        for i, ref in enumerate((a_ref, b_ref, c_ref, d_ref))
    ]
    for copy in copies:
        copy.start()
    for i, copy in enumerate(copies):
        copy.wait()
        (ab_ref if i < 2 else cd_ref)[i % 2] = held[i].astype(F32)


def state_kernel(starts_ref, k_ref, v_ref, got_ref, fk_ref, vv_ref, first_ref, *sent_refs):
    j, z = place()
    inner = unflagged(starts_ref, z + 1)
    lower = j == 0
    for h in range(HALF):
        cols = columns(j, h)
        fk_ref[0, :, head(h)] = phi(k_ref[:, cols]).astype(BF16)
        fk_ref[1, :, head(h)] = phi(got_ref[0, :, head(h)]).astype(BF16)
        vv_ref[0, :, head(h)] = v_ref[:, cols]
        vv_ref[1, :, head(h)] = got_ref[1, :, head(h)].astype(BF16)
        own, other = (dot(fk_ref[b, :, head(h)], vv_ref[b, :, head(h)], 0, 0) for b in range(2))
        first = jnp.where(lower, own, other) * inner
        first_ref[h] = first
        sent_refs[h // SIZE][h % SIZE] = jnp.where(lower, other, own) + first


def local_kernel(q_ref, got_ref, fk_ref, vv_ref, fq_ref, scores_ref, attn_ref):
    j, _ = place()
    keep = causal()
    for h in range(HALF):
        fq_ref[0, :, head(h)] = phi(q_ref[:, columns(j, h)]).astype(BF16)
        fq_ref[1, :, head(h)] = phi(got_ref[0, :, head(h)]).astype(BF16)
    for b in range(2):
        for h in range(HALF):
            raw = dot(fq_ref[b, :, head(h)], fk_ref[b, :, head(h)], 1, 1)
            scores_ref[b, h] = jnp.where(keep, raw, 0.0).astype(BF16)
    for b in range(2):
        for h in range(HALF):
            attn_ref[b, :, head(h)] = dot(scores_ref[b, h], vv_ref[b, :, head(h)], 1, 0)


def weighted(parts, weights, h):
    total = parts[0][h]
    for part, weight in zip(parts[1:], weights):
        total = total + weight * part[h]
    return total


def link_weights(starts_ref, count, nearest, step):
    weights, block, weight = [], nearest, 1.0
    for _ in range(count - 1):
        weight = weight * unflagged(starts_ref, block) * unflagged(starts_ref, block + step)
        weights.append(weight)
        block = block + 2 * step
    return weights


def norm_kernel(group, count, starts_ref, gain_ref, *refs):
    parts, refs = refs[:count], refs[count:]
    first_ref, fq_ref, c_ref, got_ref, attn_ref, state_ref, ag_ref, sent_ref, second_ref, part_ref, whole_ref = refs
    j, z = place()
    outer, inner = unflagged(starts_ref, z), unflagged(starts_ref, z + 1)
    weights = link_weights(starts_ref, count, z - 1, -1)
    lower = j == 0
    units = [(b, i) for i in range(SIZE) for b in range(2)]
    for i in range(SIZE):
        entering = outer * weighted(parts, weights, i)
        inside = inner * entering + first_ref[group * SIZE + i]
        state_ref[0, i] = jnp.where(lower, entering, inside).astype(BF16)
        state_ref[1, i] = jnp.where(lower, inside, entering).astype(BF16)
    for b, i in units:
        cols = head(group * SIZE + i)
        whole_ref[b, i] = attn_ref[b, :, cols] + dot(fq_ref[b, :, cols], state_ref[b, i], 1, 0)
    for i in range(SIZE):
        h = group * SIZE + i
        gain = gain_ref[:, columns(j, h)]
        partial = jnp.zeros((1, DH), F32)
        for b in range(2):
            attn = whole_ref[b, i]
            cot = got_ref[1, :, head(h)] if b else c_ref[:, columns(j, h)].astype(F32)
            scaled = gain * cot
            square = jnp.mean(attn * attn, axis=-1, keepdims=True)
            along = jnp.mean(attn * scaled, axis=-1, keepdims=True)
            inverse = lax.rsqrt(square + EPS)
            normed = attn * inverse
            partial = partial + jnp.sum(normed * cot, axis=0, keepdims=True)
            ag_ref[b, :, head(i)] = ((scaled - normed * (along * inverse)) * inverse).astype(BF16)
        part_ref[i : i + 1, :] = partial
    for i in range(SIZE):
        cols = head(group * SIZE + i)
        own, other = (dot(fq_ref[b, :, cols], ag_ref[b, :, head(i)], 0, 0) for b in range(2))
        second = inner * jnp.where(lower, other, own)
        second_ref[i] = second
        sent_ref[i] = jnp.where(lower, own, other) + second


def mixed_kernel(
    group, q_ref, got_ref, ag_ref, vv_ref, fk_ref, fq_ref, scores_ref, state_ref, own_ref, other_ref, kl_ref, vl_ref, mm_ref
):
    j, _ = place()
    keep = causal()
    units = [(b, i) for i in range(SIZE) for b in range(2)]
    for b, i in units:
        raw = dot(ag_ref[b, :, head(i)], vv_ref[b, :, head(group * SIZE + i)], 1, 1)
        mm_ref[b, i] = jnp.where(keep, raw, 0.0).astype(BF16)
    for b, i in units:
        vl_ref[b, :, head(i)] = dot(scores_ref[b, group * SIZE + i], ag_ref[b, :, head(i)], 0, 0)
    for b, i in units:
        cols = head(group * SIZE + i)
        part = dot(mm_ref[b, i], fk_ref[b, :, cols], 1, 0) + dot(ag_ref[b, :, head(i)], state_ref[b, i], 1, 1)
        if b:
            other_ref[:, head(i)] = part * slope(got_ref[0, :, cols])
        else:
            own_ref[:, head(i)] = (part * slope(q_ref[:, columns(j, group * SIZE + i)])).astype(BF16)
    for b, i in units:
        kl_ref[b, :, head(i)] = dot(mm_ref[b, i], fq_ref[b, :, head(group * SIZE + i)], 0, 0)


def final_kernel(group, count, starts_ref, *refs):
    parts, refs = refs[:count], refs[count:]
    k_ref, got_ref, second_ref, kl_ref, vl_ref, vv_ref, fk_ref, own_ref, other_ref, back_ref = refs
    j, z = place()
    outer, inner = unflagged(starts_ref, z + 2), unflagged(starts_ref, z + 1)
    lower = j == 0
    weights = link_weights(starts_ref, count, z + 3, 1)
    for i in range(SIZE):
        entering = outer * weighted(parts, weights, i)
        inside = inner * entering + second_ref[i]
        back_ref[0, i] = jnp.where(lower, inside, entering).astype(BF16)
        back_ref[1, i] = jnp.where(lower, entering, inside).astype(BF16)
    for i in range(SIZE):
        h = group * SIZE + i
        for b in range(2):
            key = kl_ref[b, :, head(i)] + dot(vv_ref[b, :, head(h)], back_ref[b, i], 1, 1)
            value = vl_ref[b, :, head(i)] + dot(fk_ref[b, :, head(h)], back_ref[b, i], 1, 0)
            if b:
                other_ref[0, :, head(i)] = key * slope(got_ref[0, :, head(h)])
                other_ref[1, :, head(i)] = value
            else:
                own_ref[0, :, head(i)] = (key * slope(k_ref[:, columns(j, h)])).astype(BF16)
                own_ref[1, :, head(i)] = value.astype(BF16)


def join_kernel(tokens, *refs):
    j, _ = place()
    total_ref, total_got_ref, q_ref, k_ref, v_ref, gain_ref = refs[-6:]
    root = jnp.sqrt(F32(tokens))
    gain_ref[pl.ds(pl.multiple_of(j * HALF, HALF), HALF), :] = total_ref[...] / root
    gain_ref[pl.ds(pl.multiple_of((1 - j) * HALF, HALF), HALF), :] = total_got_ref[...] / root
    for g in range(GROUPS):
        q_own_ref, q_got_ref, kv_own_ref, kv_got_ref = refs[4 * g : 4 * g + 4]
        for i in range(SIZE):
            h = g * SIZE + i
            for ref, own, got in (
                (q_ref, q_own_ref, q_got_ref),
                (k_ref, kv_own_ref.at[0], kv_got_ref.at[0]),
                (v_ref, kv_own_ref.at[1], kv_got_ref.at[1]),
            ):
                ref[:, columns(j, h)] = own[:, head(i)]
                ref[:, columns(1 - j, h)] = got[:, head(i)].astype(BF16)


VM = pl.BlockSpec(memory_space=pltpu.VMEM)
SM = pl.BlockSpec(memory_space=pltpu.SMEM)
HB = pl.BlockSpec(memory_space=pltpu.HBM)


def call(kernel, name, outs, args, scalars=0, whole=(), aliases={}, scratch=(), flops=0):
    moved = sum(a.size * a.dtype.itemsize for a in args) + sum(
        o[0][0] * functools.reduce(lambda x, y: x * y, o[0][1:], 1) * jnp.dtype(o[1]).itemsize for o in outs
    )
    return pl.pallas_call(
        kernel,
        out_shape=[jax.ShapeDtypeStruct(s, d) for s, d in outs],
        in_specs=[SM if i < scalars else HB if i in whole else VM for i in range(len(args))],
        input_output_aliases=aliases,
        out_specs=[VM] * len(outs),
        scratch_shapes=scratch,
        compiler_params=pltpu.CompilerParams(vmem_limit_bytes=24 * 1024 * 1024),
        cost_estimate=pl.CostEstimate(flops=flops, bytes_accessed=moved, transcendentals=0),
        name=name,
    )(*args)


def per_device(queries, key_rows, value_rows, out_cotangent, norm_gain, doc_starts):
    count = lax.axis_size("ctx")
    chips = count // 2
    documents = doc_starts.shape[1]
    swap = [(i, i ^ 1) for i in range(count)]
    reach = min(chips - 1, -(-(count - documents) // 2))
    q, k, v, cot = queries[0], key_rows[0], value_rows[0], out_cotangent[0]
    gain = norm_gain.reshape(1, H * DH)
    mm = 2 * HALF * 2 * SPAN * DH * DH

    def turn(x, distance):
        return lax.ppermute(x, "ctx", [(i, (i + 2 * distance) % count) for i in range(count)])

    def hop(x, distance):
        pairs = [
            (2 * i + j, 2 * (i + distance) + j)
            for i in range(chips)
            for j in range(2)
            if 0 <= i + distance < chips
        ]
        return lax.ppermute(x, "ctx", pairs)

    def arriving(sent, sign, first=None, later=None):
        if reach <= 3:
            parts = [[] for _ in sent]
            for r in range(reach):
                sent = [(turn if sign > 0 and r == 0 else hop)(x, sign) for x in sent]
                if r == 0 and first is not None:
                    at = -1 if sign > 0 else 0
                    sent[at], first = lax.optimization_barrier((sent[at], first))
                for group, x in zip(parts, sent):
                    group.append(x)
            return parts, first
        starts = doc_starts[0]
        chip = lax.axis_index("ctx") // 2

        def linked(low, high):
            return 1.0 - jnp.any((starts >= low) & (starts <= high)).astype(F32)

        distance = 1
        while distance < chips:
            if sign > 0:
                weight = linked(2 * (chip - distance) + 2, 2 * chip + 1)
            else:
                weight = linked(2 * chip + 1, 2 * (chip + distance))
            sent = [x + weight * hop(x, sign * distance) for x in sent]
            distance *= 2
        return [[hop(x, sign)] for x in sent], first

    kv_send, qc_send = call(
        pack_kernel,
        "pack",
        [((2, SPAN, WIDE), F32)] * 2,
        [pltpu.with_memory_space_constraint(x, pltpu.HBM) for x in (k, v, q, cot)],
        whole=(0, 1, 2, 3),
        scratch=[pltpu.VMEM((4, SPAN, WIDE), BF16), pltpu.SemaphoreType.DMA((4,))],
    )
    kv_got = lax.ppermute(kv_send, "ctx", swap)
    qc_got = lax.ppermute(qc_send, "ctx", swap)
    rows = ((2, SPAN, WIDE), BF16)
    wide_rows = ((2, SPAN, WIDE), F32)
    slim_rows = ((2, SPAN, SLIM), F32)
    group_square = ((SIZE, DH, DH), F32)
    group_pair = ((2, SIZE, DH, DH), BF16)
    fk, vv, first, *sent = call(
        state_kernel,
        "state",
        [rows, rows, ((HALF, DH, DH), F32)] + [group_square] * GROUPS,
        [doc_starts, k, v, kv_got],
        scalars=1,
        flops=mm,
    )
    local = call(
        local_kernel,
        "local",
        [rows, ((2, HALF, SPAN, SPAN), BF16), wide_rows],
        [q, qc_got, fk, vv],
        flops=2 * mm,
    )
    parts, local = arriving(sent, 1, local)
    fq, scores, attn = local
    normed = [
        call(
            functools.partial(norm_kernel, g, len(parts[g])),
            "norm",
            [group_pair, ((2, SPAN, SLIM), BF16), group_square, group_square, ((SIZE, DH), F32)],
            [doc_starts, gain, *parts[g], first, fq, cot, qc_got, attn],
            scalars=1,
            scratch=[pltpu.VMEM((2, SIZE, SPAN, DH), F32)],
            flops=2 * mm // GROUPS,
        )
        for g in range(GROUPS)
    ]
    dp = lax.axis_size("dp")

    def across(x, axis, low, size):
        length = lax.axis_size(axis)

        def other(y, bit):
            return lax.ppermute(y, axis, [(i, i ^ bit) for i in range(length)])

        while size > 4:
            x, low, size = x + other(x, low), 2 * low, size // 2
        if size == 2:
            return x + other(x, low)
        if size == 4:
            near, side, cross = other(x, low), other(x, 2 * low), other(x, 3 * low)
            return (x + near) + (side + cross)
        return x

    total = across(jnp.concatenate([n[4] for n in normed]), "dp", 1, dp)
    parts_back, total = arriving([n[2] for n in normed], -1, total)
    total = across(total, "ctx", 2, chips)
    joined = []
    for g in range(GROUPS):
        states, ag, _, second, _ = normed[g]
        q_own, q_send, k_local, v_local = call(
            functools.partial(mixed_kernel, g),
            "mixed",
            [((SPAN, SLIM), BF16), ((SPAN, SLIM), F32), slim_rows, slim_rows],
            [q, qc_got, ag, vv, fk, fq, scores, states],
            scratch=[pltpu.VMEM((2, SIZE, SPAN, SPAN), BF16)],
            flops=5 * mm // GROUPS,
        )
        if g == GROUPS - 1:
            second, total = lax.optimization_barrier((second, total))
        kv_own, kv_back = call(
            functools.partial(final_kernel, g, len(parts_back[g])),
            "final",
            [((2, SPAN, SLIM), BF16), slim_rows],
            [doc_starts, *parts_back[g], k, kv_got, second, k_local, v_local, vv, fk],
            scalars=1,
            scratch=[pltpu.VMEM((2, SIZE, DH, DH), BF16)],
            flops=2 * mm // GROUPS,
        )
        joined += [q_own, lax.ppermute(q_send, "ctx", swap), kv_own, lax.ppermute(kv_back, "ctx", swap)]
    total_other = lax.ppermute(total, "ctx", swap)
    query_grad, key_grad, value_grad, gain_grad = call(
        functools.partial(join_kernel, dp * SPAN * count),
        "join",
        [((SPAN, H * DH), BF16)] * 3 + [((H, DH), F32)],
        [*joined, total, total_other],
    )
    return query_grad[None], key_grad[None], value_grad[None], gain_grad.reshape(H * DH)


def solution(mesh):
    placed = (
        P("dp", "ctx", None),
        P("dp", "ctx", None),
        P("dp", "ctx", None),
        P("dp", "ctx", None),
        P(),
        P("dp", None),
    )
    return jax.shard_map(
        per_device,
        mesh=mesh,
        in_specs=placed,
        out_specs=(P("dp", "ctx", None), P("dp", "ctx", None), P("dp", "ctx", None), P()),
        check_vma=False,
    )
```

```python
import functools

import jax
import jax.numpy as jnp
from jax import lax
from jax.experimental import pallas as pl
from jax.experimental.pallas import tpu as pltpu
from jax.sharding import PartitionSpec as P

H = 16
DH = 128
SPAN = 128
HALF = H // 2
WIDE = HALF * DH
EPS = 1e-06
GROUPS = 2
SIZE = HALF // GROUPS
SLIM = SIZE * DH

F32 = jnp.float32
BF16 = jnp.bfloat16


def dot(a, b, ca, cb):
    return lax.dot_general(a, b, (((ca,), (cb,)), ((), ())), preferred_element_type=F32)


def phi(x):
    wide = x.astype(F32)
    return jnp.where(wide > 0, wide + 1.0, jnp.exp(jnp.minimum(wide, 0.0)))


def slope(x):
    wide = x.astype(F32)
    return jnp.where(wide > 0, 1.0, jnp.exp(jnp.minimum(wide, 0.0)))


def causal():
    rows = lax.broadcasted_iota(jnp.int32, (SPAN, SPAN), 0)
    cols = lax.broadcasted_iota(jnp.int32, (SPAN, SPAN), 1)
    return cols <= rows


def unflagged(starts_ref, block):
    hit = jnp.logical_or(block <= 0, block >= lax.axis_size("ctx"))
    for d in range(starts_ref.shape[1]):
        hit = jnp.logical_or(hit, starts_ref[0, d] == block)
    return jnp.where(hit, 0.0, 1.0).astype(F32)


def place():
    c = lax.axis_index("ctx")
    j = lax.rem(c, 2)
    return j, c - j


def columns(j, h):
    return pl.ds(pl.multiple_of(j * WIDE + h * DH, DH), DH)


def head(h):
    return slice(h * DH, (h + 1) * DH)


def pack_kernel(a_ref, b_ref, c_ref, d_ref, ab_ref, cd_ref, held, sems):
    j, _ = place()
    half = pl.ds(pl.multiple_of((1 - j) * WIDE, WIDE), WIDE)
    copies = [
        pltpu.make_async_copy(ref.at[:, half], held.at[i], sems.at[i])
        for i, ref in enumerate((a_ref, b_ref, c_ref, d_ref))
    ]
    for copy in copies:
        copy.start()
    for i, copy in enumerate(copies):
        copy.wait()
        (ab_ref if i < 2 else cd_ref)[i % 2] = held[i].astype(F32)


def state_kernel(starts_ref, k_ref, v_ref, got_ref, fk_ref, vv_ref, first_ref, *sent_refs):
    j, z = place()
    inner = unflagged(starts_ref, z + 1)
    lower = j == 0
    for h in range(HALF):
        cols = columns(j, h)
        fk_ref[0, :, head(h)] = phi(k_ref[:, cols]).astype(BF16)
        fk_ref[1, :, head(h)] = phi(got_ref[0, :, head(h)]).astype(BF16)
        vv_ref[0, :, head(h)] = v_ref[:, cols]
        vv_ref[1, :, head(h)] = got_ref[1, :, head(h)].astype(BF16)
        own, other = (dot(fk_ref[b, :, head(h)], vv_ref[b, :, head(h)], 0, 0) for b in range(2))
        first = jnp.where(lower, own, other) * inner
        first_ref[h] = first
        sent_refs[h // SIZE][h % SIZE] = jnp.where(lower, other, own) + first


def local_kernel(q_ref, got_ref, fk_ref, vv_ref, fq_ref, scores_ref, attn_ref):
    j, _ = place()
    keep = causal()
    for h in range(HALF):
        fq_ref[0, :, head(h)] = phi(q_ref[:, columns(j, h)]).astype(BF16)
        fq_ref[1, :, head(h)] = phi(got_ref[0, :, head(h)]).astype(BF16)
    for b in range(2):
        for h in range(HALF):
            raw = dot(fq_ref[b, :, head(h)], fk_ref[b, :, head(h)], 1, 1)
            scores_ref[b, h] = jnp.where(keep, raw, 0.0).astype(BF16)
    for b in range(2):
        for h in range(HALF):
            attn_ref[b, :, head(h)] = dot(scores_ref[b, h], vv_ref[b, :, head(h)], 1, 0)


def weighted(parts, weights, h):
    total = parts[0][h]
    for part, weight in zip(parts[1:], weights):
        total = total + weight * part[h]
    return total


def link_weights(starts_ref, count, nearest, step):
    weights, block, weight = [], nearest, 1.0
    for _ in range(count - 1):
        weight = weight * unflagged(starts_ref, block) * unflagged(starts_ref, block + step)
        weights.append(weight)
        block = block + 2 * step
    return weights


def norm_kernel(group, count, starts_ref, gain_ref, *refs):
    parts, refs = refs[:count], refs[count:]
    first_ref, fq_ref, c_ref, got_ref, attn_ref, state_ref, ag_ref, sent_ref, second_ref, part_ref, whole_ref = refs
    j, z = place()
    outer, inner = unflagged(starts_ref, z), unflagged(starts_ref, z + 1)
    weights = link_weights(starts_ref, count, z - 1, -1)
    lower = j == 0
    units = [(b, i) for i in range(SIZE) for b in range(2)]
    for i in range(SIZE):
        entering = outer * weighted(parts, weights, i)
        inside = inner * entering + first_ref[group * SIZE + i]
        state_ref[0, i] = jnp.where(lower, entering, inside).astype(BF16)
        state_ref[1, i] = jnp.where(lower, inside, entering).astype(BF16)
    for b, i in units:
        cols = head(group * SIZE + i)
        whole_ref[b, i] = attn_ref[b, :, cols] + dot(fq_ref[b, :, cols], state_ref[b, i], 1, 0)
    for i in range(SIZE):
        h = group * SIZE + i
        gain = gain_ref[:, columns(j, h)]
        partial = jnp.zeros((1, DH), F32)
        for b in range(2):
            attn = whole_ref[b, i]
            cot = got_ref[1, :, head(h)] if b else c_ref[:, columns(j, h)].astype(F32)
            scaled = gain * cot
            square = jnp.mean(attn * attn, axis=-1, keepdims=True)
            along = jnp.mean(attn * scaled, axis=-1, keepdims=True)
            inverse = lax.rsqrt(square + EPS)
            normed = attn * inverse
            partial = partial + jnp.sum(normed * cot, axis=0, keepdims=True)
            ag_ref[b, :, head(i)] = ((scaled - normed * (along * inverse)) * inverse).astype(BF16)
        part_ref[i : i + 1, :] = partial
    for i in range(SIZE):
        cols = head(group * SIZE + i)
        own, other = (dot(fq_ref[b, :, cols], ag_ref[b, :, head(i)], 0, 0) for b in range(2))
        second = inner * jnp.where(lower, other, own)
        second_ref[i] = second
        sent_ref[i] = jnp.where(lower, own, other) + second


def mixed_kernel(
    group, q_ref, got_ref, ag_ref, vv_ref, fk_ref, fq_ref, scores_ref, state_ref, own_ref, other_ref, kl_ref, vl_ref, mm_ref
):
    j, _ = place()
    keep = causal()
    units = [(b, i) for i in range(SIZE) for b in range(2)]
    for b, i in units:
        raw = dot(ag_ref[b, :, head(i)], vv_ref[b, :, head(group * SIZE + i)], 1, 1)
        mm_ref[b, i] = jnp.where(keep, raw, 0.0).astype(BF16)
    for b, i in units:
        vl_ref[b, :, head(i)] = dot(scores_ref[b, group * SIZE + i], ag_ref[b, :, head(i)], 0, 0)
    for b, i in units:
        cols = head(group * SIZE + i)
        part = dot(mm_ref[b, i], fk_ref[b, :, cols], 1, 0) + dot(ag_ref[b, :, head(i)], state_ref[b, i], 1, 1)
        if b:
            other_ref[:, head(i)] = part * slope(got_ref[0, :, cols])
        else:
            own_ref[:, head(i)] = (part * slope(q_ref[:, columns(j, group * SIZE + i)])).astype(BF16)
    for b, i in units:
        kl_ref[b, :, head(i)] = dot(mm_ref[b, i], fq_ref[b, :, head(group * SIZE + i)], 0, 0)


def final_kernel(group, count, starts_ref, *refs):
    parts, refs = refs[:count], refs[count:]
    k_ref, got_ref, second_ref, kl_ref, vl_ref, vv_ref, fk_ref, own_ref, other_ref, back_ref = refs
    j, z = place()
    outer, inner = unflagged(starts_ref, z + 2), unflagged(starts_ref, z + 1)
    lower = j == 0
    weights = link_weights(starts_ref, count, z + 3, 1)
    for i in range(SIZE):
        entering = outer * weighted(parts, weights, i)
        inside = inner * entering + second_ref[i]
        back_ref[0, i] = jnp.where(lower, inside, entering).astype(BF16)
        back_ref[1, i] = jnp.where(lower, entering, inside).astype(BF16)
    for i in range(SIZE):
        h = group * SIZE + i
        for b in range(2):
            key = kl_ref[b, :, head(i)] + dot(vv_ref[b, :, head(h)], back_ref[b, i], 1, 1)
            value = vl_ref[b, :, head(i)] + dot(fk_ref[b, :, head(h)], back_ref[b, i], 1, 0)
            if b:
                other_ref[0, :, head(i)] = key * slope(got_ref[0, :, head(h)])
                other_ref[1, :, head(i)] = value
            else:
                own_ref[0, :, head(i)] = (key * slope(k_ref[:, columns(j, h)])).astype(BF16)
                own_ref[1, :, head(i)] = value.astype(BF16)


def join_kernel(tokens, *refs):
    j, _ = place()
    total_ref, total_got_ref, q_ref, k_ref, v_ref, gain_ref = refs[-6:]
    root = jnp.sqrt(F32(tokens))
    gain_ref[pl.ds(pl.multiple_of(j * HALF, HALF), HALF), :] = total_ref[...] / root
    gain_ref[pl.ds(pl.multiple_of((1 - j) * HALF, HALF), HALF), :] = total_got_ref[...] / root
    for g in range(GROUPS):
        q_own_ref, q_got_ref, kv_own_ref, kv_got_ref = refs[4 * g : 4 * g + 4]
        for i in range(SIZE):
            h = g * SIZE + i
            for ref, own, got in (
                (q_ref, q_own_ref, q_got_ref),
                (k_ref, kv_own_ref.at[0], kv_got_ref.at[0]),
                (v_ref, kv_own_ref.at[1], kv_got_ref.at[1]),
            ):
                ref[:, columns(j, h)] = own[:, head(i)]
                ref[:, columns(1 - j, h)] = got[:, head(i)].astype(BF16)


VM = pl.BlockSpec(memory_space=pltpu.VMEM)
SM = pl.BlockSpec(memory_space=pltpu.SMEM)
HB = pl.BlockSpec(memory_space=pltpu.HBM)


def call(kernel, name, outs, args, scalars=0, whole=(), aliases={}, scratch=(), flops=0):
    moved = sum(a.size * a.dtype.itemsize for a in args) + sum(
        o[0][0] * functools.reduce(lambda x, y: x * y, o[0][1:], 1) * jnp.dtype(o[1]).itemsize for o in outs
    )
    return pl.pallas_call(
        kernel,
        out_shape=[jax.ShapeDtypeStruct(s, d) for s, d in outs],
        in_specs=[SM if i < scalars else HB if i in whole else VM for i in range(len(args))],
        input_output_aliases=aliases,
        out_specs=[VM] * len(outs),
        scratch_shapes=scratch,
        compiler_params=pltpu.CompilerParams(vmem_limit_bytes=24 * 1024 * 1024),
        cost_estimate=pl.CostEstimate(flops=flops, bytes_accessed=moved, transcendentals=0),
        name=name,
    )(*args)


def per_device(queries, key_rows, value_rows, out_cotangent, norm_gain, doc_starts):
    count = lax.axis_size("ctx")
    chips = count // 2
    documents = doc_starts.shape[1]
    swap = [(i, i ^ 1) for i in range(count)]
    reach = min(chips - 1, -(-(count - documents) // 2))
    q, k, v, cot = queries[0], key_rows[0], value_rows[0], out_cotangent[0]
    gain = norm_gain.reshape(1, H * DH)
    mm = 2 * HALF * 2 * SPAN * DH * DH

    def turn(x, distance):
        return lax.ppermute(x, "ctx", [(i, (i + 2 * distance) % count) for i in range(count)])

    def hop(x, distance):
        pairs = [
            (2 * i + j, 2 * (i + distance) + j)
            for i in range(chips)
            for j in range(2)
            if 0 <= i + distance < chips
        ]
        return lax.ppermute(x, "ctx", pairs)

    def arriving(sent, sign, first=None, later=None):
        if reach <= 3:
            parts = [[] for _ in sent]
            for r in range(reach):
                sent = [(turn if sign > 0 and r == 0 else hop)(x, sign) for x in sent]
                if r == 0 and first is not None:
                    at = -1 if sign > 0 else 0
                    sent[at], first = lax.optimization_barrier((sent[at], first))
                for group, x in zip(parts, sent):
                    group.append(x)
            return parts, first
        starts = doc_starts[0]
        chip = lax.axis_index("ctx") // 2

        def linked(low, high):
            return 1.0 - jnp.any((starts >= low) & (starts <= high)).astype(F32)

        distance = 1
        while distance < chips:
            if sign > 0:
                weight = linked(2 * (chip - distance) + 2, 2 * chip + 1)
            else:
                weight = linked(2 * chip + 1, 2 * (chip + distance))
            sent = [x + weight * hop(x, sign * distance) for x in sent]
            distance *= 2
        return [[hop(x, sign)] for x in sent], first

    kv_send, qc_send = call(
        pack_kernel,
        "pack",
        [((2, SPAN, WIDE), F32)] * 2,
        [pltpu.with_memory_space_constraint(x, pltpu.HBM) for x in (k, v, q, cot)],
        whole=(0, 1, 2, 3),
        scratch=[pltpu.VMEM((4, SPAN, WIDE), BF16), pltpu.SemaphoreType.DMA((4,))],
    )
    kv_got = lax.ppermute(kv_send, "ctx", swap)
    qc_got = lax.ppermute(qc_send, "ctx", swap)
    rows = ((2, SPAN, WIDE), BF16)
    wide_rows = ((2, SPAN, WIDE), F32)
    slim_rows = ((2, SPAN, SLIM), F32)
    group_square = ((SIZE, DH, DH), F32)
    group_pair = ((2, SIZE, DH, DH), BF16)
    fk, vv, first, *sent = call(
        state_kernel,
        "state",
        [rows, rows, ((HALF, DH, DH), F32)] + [group_square] * GROUPS,
        [doc_starts, k, v, kv_got],
        scalars=1,
        flops=mm,
    )
    local = call(
        local_kernel,
        "local",
        [rows, ((2, HALF, SPAN, SPAN), BF16), wide_rows],
        [q, qc_got, fk, vv],
        flops=2 * mm,
    )
    parts, local = arriving(sent, 1, local)
    fq, scores, attn = local
    normed = [
        call(
            functools.partial(norm_kernel, g, len(parts[g])),
            "norm" + str(g),
            [group_pair, ((2, SPAN, SLIM), BF16), group_square, group_square, ((SIZE, DH), F32)],
            [doc_starts, gain, *parts[g], first, fq, cot, qc_got, attn],
            scalars=1,
            scratch=[pltpu.VMEM((2, SIZE, SPAN, DH), F32)],
            flops=2 * mm // GROUPS,
        )
        for g in range(GROUPS)
    ]
    dp = lax.axis_size("dp")

    def across(x, axis, low, size):
        length = lax.axis_size(axis)

        def other(y, bit):
            return lax.ppermute(y, axis, [(i, i ^ bit) for i in range(length)])

        while size > (4 if axis == "ctx" else 2):
            x, low, size = x + other(x, low), 2 * low, size // 2
        if size == 2:
            return x + other(x, low)
        if size == 4:
            near, side, cross = other(x, low), other(x, 2 * low), other(x, 3 * low)
            return (x + near) + (side + cross)
        return x

    total = across(jnp.concatenate([n[4] for n in normed]), "ctx", 2, chips)
    parts_back, total = arriving([n[2] for n in normed], -1, total)

    def outputs(g):
        states, ag, _, second, _ = normed[g]
        q_own, q_send, k_local, v_local = call(
            functools.partial(mixed_kernel, g),
            "mixed" + str(g),
            [((SPAN, SLIM), BF16), ((SPAN, SLIM), F32), slim_rows, slim_rows],
            [q, qc_got, ag, vv, fk, fq, scores, states],
            scratch=[pltpu.VMEM((2, SIZE, SPAN, SPAN), BF16)],
            flops=5 * mm // GROUPS,
        )
        kv_own, kv_back = call(
            functools.partial(final_kernel, g, len(parts_back[g])),
            "final" + str(g),
            [((2, SPAN, SLIM), BF16), slim_rows],
            [doc_starts, *parts_back[g], k, kv_got, second, k_local, v_local, vv, fk],
            scalars=1,
            scratch=[pltpu.VMEM((2, SIZE, DH, DH), BF16)],
            flops=2 * mm // GROUPS,
        )
        return [q_own, q_send, kv_own, kv_back]

    done = [outputs(g) for g in range(GROUPS)]
    bit = 1
    while bit < dp:
        got = lax.ppermute(total, "dp", [(i, i ^ bit) for i in range(dp)])
        if bit == 1:
            got, done[-1] = lax.optimization_barrier((got, done[-1]))
        total = total + got
        bit *= 2
    done[0], total = lax.optimization_barrier((done[0], total))
    joined = []
    for q_own, q_send, kv_own, kv_back in done:
        joined += [q_own, lax.ppermute(q_send, "ctx", swap), kv_own, lax.ppermute(kv_back, "ctx", swap)]
    total_other = lax.ppermute(total, "ctx", swap)
    query_grad, key_grad, value_grad, gain_grad = call(
        functools.partial(join_kernel, dp * SPAN * count),
        "join",
        [((SPAN, H * DH), BF16)] * 3 + [((H, DH), F32)],
        [*joined, total, total_other],
    )
    return query_grad[None], key_grad[None], value_grad[None], gain_grad.reshape(H * DH)


def solution(mesh):
    placed = (
        P("dp", "ctx", None),
        P("dp", "ctx", None),
        P("dp", "ctx", None),
        P("dp", "ctx", None),
        P(),
        P("dp", None),
    )
    return jax.shard_map(
        per_device,
        mesh=mesh,
        in_specs=placed,
        out_specs=(P("dp", "ctx", None), P("dp", "ctx", None), P("dp", "ctx", None), P()),
        check_vma=False,
    )
```

```python
import functools

import jax
import jax.numpy as jnp
from jax import lax
from jax.experimental import pallas as pl
from jax.experimental.pallas import tpu as pltpu
from jax.sharding import PartitionSpec as P

H = 16
DH = 128
SPAN = 128
HALF = H // 2
WIDE = HALF * DH
EPS = 1e-06
GROUPS = 2
SIZE = HALF // GROUPS
SLIM = SIZE * DH

F32 = jnp.float32
BF16 = jnp.bfloat16


def dot(a, b, ca, cb):
    return lax.dot_general(a, b, (((ca,), (cb,)), ((), ())), preferred_element_type=F32)


def phi(x):
    wide = x.astype(F32)
    return jnp.where(wide > 0, wide + 1.0, jnp.exp(jnp.minimum(wide, 0.0)))


def slope(x):
    wide = x.astype(F32)
    return jnp.where(wide > 0, 1.0, jnp.exp(jnp.minimum(wide, 0.0)))


def causal():
    rows = lax.broadcasted_iota(jnp.int32, (SPAN, SPAN), 0)
    cols = lax.broadcasted_iota(jnp.int32, (SPAN, SPAN), 1)
    return cols <= rows


def unflagged(starts_ref, block):
    hit = jnp.logical_or(block <= 0, block >= lax.axis_size("ctx"))
    for d in range(starts_ref.shape[1]):
        hit = jnp.logical_or(hit, starts_ref[0, d] == block)
    return jnp.where(hit, 0.0, 1.0).astype(F32)


def place():
    c = lax.axis_index("ctx")
    j = lax.rem(c, 2)
    return j, c - j


def columns(j, h):
    return pl.ds(pl.multiple_of(j * WIDE + h * DH, DH), DH)


def head(h):
    return slice(h * DH, (h + 1) * DH)


def pack_kernel(pieces, count, *refs):
    j, _ = place()
    ins, outs = refs[:count], refs[count : count + len(pieces)]
    held, sems = refs[count + len(pieces) : -1], refs[-1]
    copies = []
    for p, (pair, start, wide) in enumerate(pieces):
        cols = pl.ds(pl.multiple_of((1 - j) * WIDE + start, DH), wide)
        for side in range(2):
            source = ins[2 * pair + side].at[:, cols]
            copies.append(pltpu.make_async_copy(source, held[p].at[side], sems.at[2 * p + side]))
    for copy in copies:
        copy.start()
    for p in range(len(pieces)):
        for side in range(2):
            copies[2 * p + side].wait()
            outs[p][side] = held[p][side].astype(F32)


def state_kernel(group, starts_ref, k_ref, v_ref, got_ref, fk_ref, vv_ref, first_ref, sent_ref):
    j, z = place()
    inner = unflagged(starts_ref, z + 1)
    lower = j == 0
    for i in range(SIZE):
        cols = columns(j, group * SIZE + i)
        fk_ref[0, :, head(i)] = phi(k_ref[:, cols]).astype(BF16)
        fk_ref[1, :, head(i)] = phi(got_ref[0, :, head(i)]).astype(BF16)
        vv_ref[0, :, head(i)] = v_ref[:, cols]
        vv_ref[1, :, head(i)] = got_ref[1, :, head(i)].astype(BF16)
    for i in range(SIZE):
        own, other = (dot(fk_ref[b, :, head(i)], vv_ref[b, :, head(i)], 0, 0) for b in range(2))
        first = jnp.where(lower, own, other) * inner
        first_ref[i] = first
        sent_ref[i] = jnp.where(lower, other, own) + first


def local_kernel(q_ref, got_ref, *refs):
    features, (fq_ref, scores_ref, attn_ref) = refs[:-3], refs[-3:]
    j, _ = place()
    keep = causal()
    units = [(b, g, i) for b in range(2) for g in range(GROUPS) for i in range(SIZE)]
    for h in range(HALF):
        fq_ref[0, :, head(h)] = phi(q_ref[:, columns(j, h)]).astype(BF16)
        fq_ref[1, :, head(h)] = phi(got_ref[0, :, head(h)]).astype(BF16)
    for b, g, i in units:
        h = g * SIZE + i
        raw = dot(fq_ref[b, :, head(h)], features[2 * g][b, :, head(i)], 1, 1)
        scores_ref[b, h] = jnp.where(keep, raw, 0.0).astype(BF16)
    for b, g, i in units:
        h = g * SIZE + i
        attn_ref[b, :, head(h)] = dot(scores_ref[b, h], features[2 * g + 1][b, :, head(i)], 1, 0)


def weighted(parts, weights, h):
    total = parts[0][h]
    for part, weight in zip(parts[1:], weights):
        total = total + weight * part[h]
    return total


def link_weights(starts_ref, count, nearest, step):
    weights, block, weight = [], nearest, 1.0
    for _ in range(count - 1):
        weight = weight * unflagged(starts_ref, block) * unflagged(starts_ref, block + step)
        weights.append(weight)
        block = block + 2 * step
    return weights


def norm_kernel(group, count, starts_ref, gain_ref, *refs):
    parts, refs = refs[:count], refs[count:]
    first_ref, fq_ref, c_ref, got_ref, attn_ref, state_ref, ag_ref, sent_ref, second_ref, part_ref, whole_ref = refs
    j, z = place()
    outer, inner = unflagged(starts_ref, z), unflagged(starts_ref, z + 1)
    weights = link_weights(starts_ref, count, z - 1, -1)
    lower = j == 0
    units = [(b, i) for i in range(SIZE) for b in range(2)]
    for i in range(SIZE):
        entering = outer * weighted(parts, weights, i)
        inside = inner * entering + first_ref[i]
        state_ref[0, i] = jnp.where(lower, entering, inside).astype(BF16)
        state_ref[1, i] = jnp.where(lower, inside, entering).astype(BF16)
    for b, i in units:
        cols = head(group * SIZE + i)
        whole_ref[b, i] = attn_ref[b, :, cols] + dot(fq_ref[b, :, cols], state_ref[b, i], 1, 0)
    for i in range(SIZE):
        h = group * SIZE + i
        gain = gain_ref[:, columns(j, h)]
        partial = jnp.zeros((1, DH), F32)
        for b in range(2):
            attn = whole_ref[b, i]
            cot = got_ref[1, :, head(h)] if b else c_ref[:, columns(j, h)].astype(F32)
            scaled = gain * cot
            square = jnp.mean(attn * attn, axis=-1, keepdims=True)
            along = jnp.mean(attn * scaled, axis=-1, keepdims=True)
            inverse = lax.rsqrt(square + EPS)
            normed = attn * inverse
            partial = partial + jnp.sum(normed * cot, axis=0, keepdims=True)
            ag_ref[b, :, head(i)] = ((scaled - normed * (along * inverse)) * inverse).astype(BF16)
        part_ref[i : i + 1, :] = partial
    for i in range(SIZE):
        cols = head(group * SIZE + i)
        own, other = (dot(fq_ref[b, :, cols], ag_ref[b, :, head(i)], 0, 0) for b in range(2))
        second = inner * jnp.where(lower, other, own)
        second_ref[i] = second
        sent_ref[i] = jnp.where(lower, own, other) + second


def mixed_kernel(
    group, q_ref, got_ref, ag_ref, vv_ref, fk_ref, fq_ref, scores_ref, state_ref, own_ref, other_ref, kl_ref, vl_ref, mm_ref
):
    j, _ = place()
    keep = causal()
    units = [(b, i) for i in range(SIZE) for b in range(2)]
    for b, i in units:
        raw = dot(ag_ref[b, :, head(i)], vv_ref[b, :, head(i)], 1, 1)
        mm_ref[b, i] = jnp.where(keep, raw, 0.0).astype(BF16)
    for b, i in units:
        vl_ref[b, :, head(i)] = dot(scores_ref[b, group * SIZE + i], ag_ref[b, :, head(i)], 0, 0)
    for b, i in units:
        cols = head(group * SIZE + i)
        part = dot(mm_ref[b, i], fk_ref[b, :, head(i)], 1, 0) + dot(ag_ref[b, :, head(i)], state_ref[b, i], 1, 1)
        if b:
            other_ref[:, head(i)] = part * slope(got_ref[0, :, cols])
        else:
            own_ref[:, head(i)] = (part * slope(q_ref[:, columns(j, group * SIZE + i)])).astype(BF16)
    for b, i in units:
        kl_ref[b, :, head(i)] = dot(mm_ref[b, i], fq_ref[b, :, head(group * SIZE + i)], 0, 0)


def final_kernel(group, count, starts_ref, *refs):
    parts, refs = refs[:count], refs[count:]
    k_ref, got_ref, second_ref, kl_ref, vl_ref, vv_ref, fk_ref, own_ref, other_ref, back_ref = refs
    j, z = place()
    outer, inner = unflagged(starts_ref, z + 2), unflagged(starts_ref, z + 1)
    lower = j == 0
    weights = link_weights(starts_ref, count, z + 3, 1)
    for i in range(SIZE):
        entering = outer * weighted(parts, weights, i)
        inside = inner * entering + second_ref[i]
        back_ref[0, i] = jnp.where(lower, inside, entering).astype(BF16)
        back_ref[1, i] = jnp.where(lower, entering, inside).astype(BF16)
    for i in range(SIZE):
        h = group * SIZE + i
        for b in range(2):
            key = kl_ref[b, :, head(i)] + dot(vv_ref[b, :, head(i)], back_ref[b, i], 1, 1)
            value = vl_ref[b, :, head(i)] + dot(fk_ref[b, :, head(i)], back_ref[b, i], 1, 0)
            if b:
                other_ref[0, :, head(i)] = key * slope(got_ref[0, :, head(i)])
                other_ref[1, :, head(i)] = value
            else:
                own_ref[0, :, head(i)] = (key * slope(k_ref[:, columns(j, h)])).astype(BF16)
                own_ref[1, :, head(i)] = value.astype(BF16)


def join_kernel(tokens, *refs):
    j, _ = place()
    total_ref, total_got_ref, q_ref, k_ref, v_ref, gain_ref = refs[-6:]
    root = jnp.sqrt(F32(tokens))
    gain_ref[pl.ds(pl.multiple_of(j * HALF, HALF), HALF), :] = total_ref[...] / root
    gain_ref[pl.ds(pl.multiple_of((1 - j) * HALF, HALF), HALF), :] = total_got_ref[...] / root
    for g in range(GROUPS):
        q_own_ref, q_got_ref, kv_own_ref, kv_got_ref = refs[4 * g : 4 * g + 4]
        for i in range(SIZE):
            h = g * SIZE + i
            for ref, own, got in (
                (q_ref, q_own_ref, q_got_ref),
                (k_ref, kv_own_ref.at[0], kv_got_ref.at[0]),
                (v_ref, kv_own_ref.at[1], kv_got_ref.at[1]),
            ):
                ref[:, columns(j, h)] = own[:, head(i)]
                ref[:, columns(1 - j, h)] = got[:, head(i)].astype(BF16)


VM = pl.BlockSpec(memory_space=pltpu.VMEM)
SM = pl.BlockSpec(memory_space=pltpu.SMEM)
HB = pl.BlockSpec(memory_space=pltpu.HBM)


def call(kernel, name, outs, args, scalars=0, whole=(), aliases={}, scratch=(), flops=0):
    moved = sum(a.size * a.dtype.itemsize for a in args) + sum(
        o[0][0] * functools.reduce(lambda x, y: x * y, o[0][1:], 1) * jnp.dtype(o[1]).itemsize for o in outs
    )
    return pl.pallas_call(
        kernel,
        out_shape=[jax.ShapeDtypeStruct(s, d) for s, d in outs],
        in_specs=[SM if i < scalars else HB if i in whole else VM for i in range(len(args))],
        input_output_aliases=aliases,
        out_specs=[VM] * len(outs),
        scratch_shapes=scratch,
        compiler_params=pltpu.CompilerParams(vmem_limit_bytes=24 * 1024 * 1024),
        cost_estimate=pl.CostEstimate(flops=flops, bytes_accessed=moved, transcendentals=0),
        name=name,
    )(*args)


def per_device(queries, key_rows, value_rows, out_cotangent, norm_gain, doc_starts):
    count = lax.axis_size("ctx")
    chips = count // 2
    documents = doc_starts.shape[1]
    swap = [(i, i ^ 1) for i in range(count)]
    reach = min(chips - 1, -(-(count - documents) // 2))
    q, k, v, cot = queries[0], key_rows[0], value_rows[0], out_cotangent[0]
    gain = norm_gain.reshape(1, H * DH)
    mm = 2 * HALF * 2 * SPAN * DH * DH

    def turn(x, distance):
        return lax.ppermute(x, "ctx", [(i, (i + 2 * distance) % count) for i in range(count)])

    def hop(x, distance):
        pairs = [
            (2 * i + j, 2 * (i + distance) + j)
            for i in range(chips)
            for j in range(2)
            if 0 <= i + distance < chips
        ]
        return lax.ppermute(x, "ctx", pairs)

    def arriving(sent, sign, first=None, later=None):
        if reach <= 3:
            parts = [[] for _ in sent]
            for r in range(reach):
                sent = [(turn if sign > 0 and r == 0 else hop)(x, sign) for x in sent]
                if r == 0 and first is not None:
                    at = -1 if sign > 0 else 0
                    sent[at], first = lax.optimization_barrier((sent[at], first))
                for group, x in zip(parts, sent):
                    group.append(x)
            return parts, first
        starts = doc_starts[0]
        chip = lax.axis_index("ctx") // 2

        def linked(low, high):
            return 1.0 - jnp.any((starts >= low) & (starts <= high)).astype(F32)

        distance = 1
        while distance < chips:
            if sign > 0:
                weight = linked(2 * (chip - distance) + 2, 2 * chip + 1)
            else:
                weight = linked(2 * chip + 1, 2 * (chip + distance))
            sent = [x + weight * hop(x, sign * distance) for x in sent]
            distance *= 2
        return [[hop(x, sign)] for x in sent], first

    order = list(range(GROUPS))[::-1]
    pieces = [(0, g * SLIM, SLIM) for g in order] + [(1, 0, WIDE)]
    *kv_send, qc_send = call(
        functools.partial(pack_kernel, pieces, 4),
        "pack",
        [((2, SPAN, wide), F32) for _, _, wide in pieces],
        [pltpu.with_memory_space_constraint(x, pltpu.HBM) for x in (k, v, q, cot)],
        whole=range(4),
        scratch=[pltpu.VMEM((2, SPAN, wide), BF16) for _, _, wide in pieces]
        + [pltpu.SemaphoreType.DMA((2 * len(pieces),))],
    )
    ahead = lax.ppermute(kv_send[0], "ctx", swap)
    ahead, kv_send, qc_send = lax.optimization_barrier((ahead, kv_send[1:], qc_send))
    kv_got = [ahead, *(lax.ppermute(x, "ctx", swap) for x in kv_send)][::-1]
    qc_got = lax.ppermute(qc_send, "ctx", swap)
    mm = 2 * HALF * 2 * SPAN * DH * DH
    rows = ((2, SPAN, WIDE), BF16)
    wide_rows = ((2, SPAN, WIDE), F32)
    slim_rows = ((2, SPAN, SLIM), F32)
    group_square = ((SIZE, DH, DH), F32)
    group_pair = ((2, SIZE, DH, DH), BF16)
    slim = ((2, SPAN, SLIM), BF16)
    made = [
        call(
            functools.partial(state_kernel, g),
            "state" + str(g),
            [slim, slim, group_square, group_square],
            [doc_starts, k, v, kv_got[g]],
            scalars=1,
            flops=mm // GROUPS,
        )
        for g in range(GROUPS)
    ]
    sent = [m[3] for m in made]
    local = call(
        local_kernel,
        "local",
        [rows, ((2, HALF, SPAN, SPAN), BF16), wide_rows],
        [q, qc_got] + [x for m in made for x in m[:2]],
        flops=2 * mm,
    )
    parts, local = arriving(sent, 1, local)
    fq, scores, attn = local
    normed = [
        call(
            functools.partial(norm_kernel, g, len(parts[g])),
            "norm" + str(g),
            [group_pair, ((2, SPAN, SLIM), BF16), group_square, group_square, ((SIZE, DH), F32)],
            [doc_starts, gain, *parts[g], made[g][2], fq, cot, qc_got, attn],
            scalars=1,
            scratch=[pltpu.VMEM((2, SIZE, SPAN, DH), F32)],
            flops=2 * mm // GROUPS,
        )
        for g in range(GROUPS)
    ]
    dp = lax.axis_size("dp")

    def across(x, axis, low, size):
        length = lax.axis_size(axis)

        def other(y, bit):
            return lax.ppermute(y, axis, [(i, i ^ bit) for i in range(length)])

        while size > (4 if axis == "ctx" else 2):
            x, low, size = x + other(x, low), 2 * low, size // 2
        if size == 2:
            return x + other(x, low)
        if size == 4:
            near, side, cross = other(x, low), other(x, 2 * low), other(x, 3 * low)
            return (x + near) + (side + cross)
        return x

    total = across(jnp.concatenate([n[4] for n in normed]), "ctx", 2, chips)
    parts_back, total = arriving([n[2] for n in normed], -1, total)

    def outputs(g):
        states, ag, _, second, _ = normed[g]
        fk, vv = made[g][:2]
        q_own, q_send, k_local, v_local = call(
            functools.partial(mixed_kernel, g),
            "mixed" + str(g),
            [((SPAN, SLIM), BF16), ((SPAN, SLIM), F32), slim_rows, slim_rows],
            [q, qc_got, ag, vv, fk, fq, scores, states],
            scratch=[pltpu.VMEM((2, SIZE, SPAN, SPAN), BF16)],
            flops=5 * mm // GROUPS,
        )
        kv_own, kv_back = call(
            functools.partial(final_kernel, g, len(parts_back[g])),
            "final" + str(g),
            [((2, SPAN, SLIM), BF16), slim_rows],
            [doc_starts, *parts_back[g], k, kv_got[g], second, k_local, v_local, vv, fk],
            scalars=1,
            scratch=[pltpu.VMEM((2, SIZE, DH, DH), BF16)],
            flops=2 * mm // GROUPS,
        )
        return [q_own, q_send, kv_own, kv_back]

    done = [outputs(g) for g in range(GROUPS)]
    bit = 1
    while bit < dp:
        got = lax.ppermute(total, "dp", [(i, i ^ bit) for i in range(dp)])
        if bit == 1:
            got, done[-1] = lax.optimization_barrier((got, done[-1]))
        total = total + got
        bit *= 2
    done[0], total = lax.optimization_barrier((done[0], total))
    joined = []
    for q_own, q_send, kv_own, kv_back in done:
        joined += [q_own, lax.ppermute(q_send, "ctx", swap), kv_own, lax.ppermute(kv_back, "ctx", swap)]
    total_other = lax.ppermute(total, "ctx", swap)
    query_grad, key_grad, value_grad, gain_grad = call(
        functools.partial(join_kernel, dp * SPAN * count),
        "join",
        [((SPAN, H * DH), BF16)] * 3 + [((H, DH), F32)],
        [*joined, total, total_other],
    )
    return query_grad[None], key_grad[None], value_grad[None], gain_grad.reshape(H * DH)


def solution(mesh):
    placed = (
        P("dp", "ctx", None),
        P("dp", "ctx", None),
        P("dp", "ctx", None),
        P("dp", "ctx", None),
        P(),
        P("dp", None),
    )
    return jax.shard_map(
        per_device,
        mesh=mesh,
        in_specs=placed,
        out_specs=(P("dp", "ctx", None), P("dp", "ctx", None), P("dp", "ctx", None), P()),
        check_vma=False,
    )
```

```python
import functools

import jax
import jax.numpy as jnp
from jax import lax
from jax.experimental import pallas as pl
from jax.experimental.pallas import tpu as pltpu
from jax.sharding import PartitionSpec as P

H = 16
DH = 128
SPAN = 128
HALF = H // 2
WIDE = HALF * DH
EPS = 1e-06
GROUPS = 2
SIZE = HALF // GROUPS
SLIM = SIZE * DH

F32 = jnp.float32
BF16 = jnp.bfloat16


def dot(a, b, ca, cb):
    return lax.dot_general(a, b, (((ca,), (cb,)), ((), ())), preferred_element_type=F32)


def phi(x):
    wide = x.astype(F32)
    return jnp.where(wide > 0, wide + 1.0, jnp.exp(jnp.minimum(wide, 0.0)))


def slope(x):
    wide = x.astype(F32)
    return jnp.where(wide > 0, 1.0, jnp.exp(jnp.minimum(wide, 0.0)))


def causal():
    rows = lax.broadcasted_iota(jnp.int32, (SPAN, SPAN), 0)
    cols = lax.broadcasted_iota(jnp.int32, (SPAN, SPAN), 1)
    return cols <= rows


def unflagged(starts_ref, block):
    hit = jnp.logical_or(block <= 0, block >= lax.axis_size("ctx"))
    for d in range(starts_ref.shape[1]):
        hit = jnp.logical_or(hit, starts_ref[0, d] == block)
    return jnp.where(hit, 0.0, 1.0).astype(F32)


def place():
    c = lax.axis_index("ctx")
    j = lax.rem(c, 2)
    return j, c - j


def columns(j, h):
    return pl.ds(pl.multiple_of(j * WIDE + h * DH, DH), DH)


def head(h):
    return slice(h * DH, (h + 1) * DH)


def pack_kernel(pieces, count, *refs):
    j, _ = place()
    ins, outs = refs[:count], refs[count : count + len(pieces)]
    held, sems = refs[count + len(pieces) : -1], refs[-1]
    copies = []
    for p, (pair, start, wide) in enumerate(pieces):
        cols = pl.ds(pl.multiple_of((1 - j) * WIDE + start, DH), wide)
        for side in range(2):
            source = ins[2 * pair + side].at[:, cols]
            copies.append(pltpu.make_async_copy(source, held[p].at[side], sems.at[2 * p + side]))
    for copy in copies:
        copy.start()
    for p in range(len(pieces)):
        for side in range(2):
            copies[2 * p + side].wait()
            outs[p][side] = held[p][side].astype(F32)


def state_kernel(group, starts_ref, k_ref, v_ref, got_ref, fk_ref, vv_ref, first_ref, sent_ref):
    j, z = place()
    inner = unflagged(starts_ref, z + 1)
    lower = j == 0
    for i in range(SIZE):
        cols = columns(j, group * SIZE + i)
        fk_ref[0, :, head(i)] = phi(k_ref[:, cols]).astype(BF16)
        fk_ref[1, :, head(i)] = phi(got_ref[0, :, head(i)]).astype(BF16)
        vv_ref[0, :, head(i)] = v_ref[:, cols]
        vv_ref[1, :, head(i)] = got_ref[1, :, head(i)].astype(BF16)
    for i in range(SIZE):
        own, other = (dot(fk_ref[b, :, head(i)], vv_ref[b, :, head(i)], 0, 0) for b in range(2))
        first = jnp.where(lower, own, other) * inner
        first_ref[i] = first
        sent_ref[i] = jnp.where(lower, other, own) + first


def local_kernel(q_ref, got_ref, *refs):
    features, (fq_ref, scores_ref, attn_ref) = refs[:-3], refs[-3:]
    j, _ = place()
    keep = causal()
    units = [(b, g, i) for b in range(2) for g in range(GROUPS) for i in range(SIZE)]
    for h in range(HALF):
        fq_ref[0, :, head(h)] = phi(q_ref[:, columns(j, h)]).astype(BF16)
        fq_ref[1, :, head(h)] = phi(got_ref[0, :, head(h)]).astype(BF16)
    for b, g, i in units:
        h = g * SIZE + i
        raw = dot(fq_ref[b, :, head(h)], features[2 * g][b, :, head(i)], 1, 1)
        scores_ref[b, h] = jnp.where(keep, raw, 0.0).astype(BF16)
    for b, g, i in units:
        h = g * SIZE + i
        attn_ref[b, :, head(h)] = dot(scores_ref[b, h], features[2 * g + 1][b, :, head(i)], 1, 0)


def weighted(parts, weights, h):
    total = parts[0][h]
    for part, weight in zip(parts[1:], weights):
        total = total + weight * part[h]
    return total


def link_weights(starts_ref, count, nearest, step):
    weights, block, weight = [], nearest, 1.0
    for _ in range(count - 1):
        weight = weight * unflagged(starts_ref, block) * unflagged(starts_ref, block + step)
        weights.append(weight)
        block = block + 2 * step
    return weights


def norm_kernel(group, count, starts_ref, gain_ref, *refs):
    parts, refs = refs[:count], refs[count:]
    first_ref, fq_ref, c_ref, got_ref, attn_ref, state_ref, ag_ref, sent_ref, second_ref, part_ref, whole_ref = refs
    j, z = place()
    outer, inner = unflagged(starts_ref, z), unflagged(starts_ref, z + 1)
    weights = link_weights(starts_ref, count, z - 1, -1)
    lower = j == 0
    units = [(b, i) for i in range(SIZE) for b in range(2)]
    for i in range(SIZE):
        entering = outer * weighted(parts, weights, i)
        inside = inner * entering + first_ref[i]
        state_ref[0, i] = jnp.where(lower, entering, inside).astype(BF16)
        state_ref[1, i] = jnp.where(lower, inside, entering).astype(BF16)
    for b, i in units:
        cols = head(group * SIZE + i)
        whole_ref[b, i] = attn_ref[b, :, cols] + dot(fq_ref[b, :, cols], state_ref[b, i], 1, 0)
    for i in range(SIZE):
        h = group * SIZE + i
        gain = gain_ref[:, columns(j, h)]
        partial = jnp.zeros((1, DH), F32)
        for b in range(2):
            attn = whole_ref[b, i]
            cot = got_ref[1, :, head(h)] if b else c_ref[:, columns(j, h)].astype(F32)
            scaled = gain * cot
            square = jnp.mean(attn * attn, axis=-1, keepdims=True)
            along = jnp.mean(attn * scaled, axis=-1, keepdims=True)
            inverse = lax.rsqrt(square + EPS)
            normed = attn * inverse
            partial = partial + jnp.sum(normed * cot, axis=0, keepdims=True)
            ag_ref[b, :, head(i)] = ((scaled - normed * (along * inverse)) * inverse).astype(BF16)
        part_ref[i : i + 1, :] = partial
    for i in range(SIZE):
        cols = head(group * SIZE + i)
        own, other = (dot(fq_ref[b, :, cols], ag_ref[b, :, head(i)], 0, 0) for b in range(2))
        second = inner * jnp.where(lower, other, own)
        second_ref[i] = second
        sent_ref[i] = jnp.where(lower, own, other) + second


def mixed_kernel(
    group, q_ref, got_ref, ag_ref, vv_ref, fk_ref, fq_ref, scores_ref, state_ref, own_ref, other_ref, kl_ref, vl_ref, mm_ref
):
    j, _ = place()
    keep = causal()
    units = [(b, i) for i in range(SIZE) for b in range(2)]
    for b, i in units:
        raw = dot(ag_ref[b, :, head(i)], vv_ref[b, :, head(i)], 1, 1)
        mm_ref[b, i] = jnp.where(keep, raw, 0.0).astype(BF16)
    for b, i in units:
        vl_ref[b, :, head(i)] = dot(scores_ref[b, group * SIZE + i], ag_ref[b, :, head(i)], 0, 0)
    for b, i in units:
        cols = head(group * SIZE + i)
        part = dot(mm_ref[b, i], fk_ref[b, :, head(i)], 1, 0) + dot(ag_ref[b, :, head(i)], state_ref[b, i], 1, 1)
        if b:
            other_ref[:, head(i)] = part * slope(got_ref[0, :, cols])
        else:
            own_ref[:, head(i)] = (part * slope(q_ref[:, columns(j, group * SIZE + i)])).astype(BF16)
    for b, i in units:
        kl_ref[b, :, head(i)] = dot(mm_ref[b, i], fq_ref[b, :, head(group * SIZE + i)], 0, 0)


def final_kernel(group, count, extras, starts_ref, *refs):
    parts, more, refs = refs[:count], refs[count : count + extras], refs[count + extras :]
    k_ref, got_ref, second_ref, kl_ref, vl_ref, vv_ref, fk_ref, own_ref, other_ref, back_ref = refs
    j, z = place()
    outer, inner = unflagged(starts_ref, z + 2), unflagged(starts_ref, z + 1)
    lower = j == 0
    weights = link_weights(starts_ref, count, z + 3, 1)
    for e in range(extras):
        other_ref[e] = more[e][...]
    for i in range(SIZE):
        entering = outer * weighted(parts, weights, i)
        inside = inner * entering + second_ref[i]
        back_ref[0, i] = jnp.where(lower, inside, entering).astype(BF16)
        back_ref[1, i] = jnp.where(lower, entering, inside).astype(BF16)
    for i in range(SIZE):
        h = group * SIZE + i
        for b in range(2):
            key = kl_ref[b, :, head(i)] + dot(vv_ref[b, :, head(i)], back_ref[b, i], 1, 1)
            value = vl_ref[b, :, head(i)] + dot(fk_ref[b, :, head(i)], back_ref[b, i], 1, 0)
            if b:
                other_ref[extras, :, head(i)] = key * slope(got_ref[0, :, head(i)])
                other_ref[extras + 1, :, head(i)] = value
            else:
                own_ref[0, :, head(i)] = (key * slope(k_ref[:, columns(j, h)])).astype(BF16)
                own_ref[1, :, head(i)] = value.astype(BF16)


def join_kernel(tokens, *refs):
    j, _ = place()
    total_ref, total_got_ref, q_ref, k_ref, v_ref, gain_ref = refs[-6:]
    root = jnp.sqrt(F32(tokens))
    gain_ref[pl.ds(pl.multiple_of(j * HALF, HALF), HALF), :] = total_ref[...] / root
    gain_ref[pl.ds(pl.multiple_of((1 - j) * HALF, HALF), HALF), :] = total_got_ref[...] / root
    for g in range(GROUPS):
        kv_own_ref, kv_got_ref = refs[GROUPS + 2 * g : GROUPS + 2 * g + 2]
        for i in range(SIZE):
            h = g * SIZE + i
            for ref, own, got in (
                (q_ref, refs[g], kv_got_ref.at[0]),
                (k_ref, kv_own_ref.at[0], kv_got_ref.at[1]),
                (v_ref, kv_own_ref.at[1], kv_got_ref.at[2]),
            ):
                ref[:, columns(j, h)] = own[:, head(i)]
                ref[:, columns(1 - j, h)] = got[:, head(i)].astype(BF16)


VM = pl.BlockSpec(memory_space=pltpu.VMEM)
SM = pl.BlockSpec(memory_space=pltpu.SMEM)
HB = pl.BlockSpec(memory_space=pltpu.HBM)


def call(kernel, name, outs, args, scalars=0, whole=(), aliases={}, scratch=(), flops=0):
    moved = sum(a.size * a.dtype.itemsize for a in args) + sum(
        o[0][0] * functools.reduce(lambda x, y: x * y, o[0][1:], 1) * jnp.dtype(o[1]).itemsize for o in outs
    )
    return pl.pallas_call(
        kernel,
        out_shape=[jax.ShapeDtypeStruct(s, d) for s, d in outs],
        in_specs=[SM if i < scalars else HB if i in whole else VM for i in range(len(args))],
        input_output_aliases=aliases,
        out_specs=[VM] * len(outs),
        scratch_shapes=scratch,
        compiler_params=pltpu.CompilerParams(vmem_limit_bytes=24 * 1024 * 1024),
        cost_estimate=pl.CostEstimate(flops=flops, bytes_accessed=moved, transcendentals=0),
        name=name,
    )(*args)


def per_device(queries, key_rows, value_rows, out_cotangent, norm_gain, doc_starts):
    count = lax.axis_size("ctx")
    chips = count // 2
    documents = doc_starts.shape[1]
    swap = [(i, i ^ 1) for i in range(count)]
    reach = min(chips - 1, -(-(count - documents) // 2))
    q, k, v, cot = queries[0], key_rows[0], value_rows[0], out_cotangent[0]
    gain = norm_gain.reshape(1, H * DH)
    mm = 2 * HALF * 2 * SPAN * DH * DH

    def turn(x, distance):
        return lax.ppermute(x, "ctx", [(i, (i + 2 * distance) % count) for i in range(count)])

    def hop(x, distance):
        pairs = [
            (2 * i + j, 2 * (i + distance) + j)
            for i in range(chips)
            for j in range(2)
            if 0 <= i + distance < chips
        ]
        return lax.ppermute(x, "ctx", pairs)

    def arriving(sent, sign, first=None, later=None):
        if reach <= 3:
            parts = [[] for _ in sent]
            for r in range(reach):
                sent = [(turn if (sign > 0) == (r == 0) else hop)(x, sign) for x in sent]
                if r == 0 and first is not None:
                    at = -1 if sign > 0 else 0
                    sent[at], first = lax.optimization_barrier((sent[at], first))
                for group, x in zip(parts, sent):
                    group.append(x)
            return parts, first
        starts = doc_starts[0]
        chip = lax.axis_index("ctx") // 2

        def linked(low, high):
            return 1.0 - jnp.any((starts >= low) & (starts <= high)).astype(F32)

        distance = 1
        while distance < chips:
            if sign > 0:
                weight = linked(2 * (chip - distance) + 2, 2 * chip + 1)
            else:
                weight = linked(2 * chip + 1, 2 * (chip + distance))
            sent = [x + weight * hop(x, sign * distance) for x in sent]
            distance *= 2
        return [[hop(x, sign)] for x in sent], first

    order = list(range(GROUPS))[::-1]
    pieces = [(0, g * SLIM, SLIM) for g in order] + [(1, 0, WIDE)]
    *kv_send, qc_send = call(
        functools.partial(pack_kernel, pieces, 4),
        "pack",
        [((2, SPAN, wide), F32) for _, _, wide in pieces],
        [pltpu.with_memory_space_constraint(x, pltpu.HBM) for x in (k, v, q, cot)],
        whole=range(4),
        scratch=[pltpu.VMEM((2, SPAN, wide), BF16) for _, _, wide in pieces]
        + [pltpu.SemaphoreType.DMA((2 * len(pieces),))],
    )
    ahead = lax.ppermute(kv_send[0], "ctx", swap)
    ahead, kv_send, qc_send = lax.optimization_barrier((ahead, kv_send[1:], qc_send))
    kv_got = [ahead, *(lax.ppermute(x, "ctx", swap) for x in kv_send)][::-1]
    qc_got = lax.ppermute(qc_send, "ctx", swap)
    mm = 2 * HALF * 2 * SPAN * DH * DH
    rows = ((2, SPAN, WIDE), BF16)
    wide_rows = ((2, SPAN, WIDE), F32)
    slim_rows = ((2, SPAN, SLIM), F32)
    group_square = ((SIZE, DH, DH), F32)
    group_pair = ((2, SIZE, DH, DH), BF16)
    slim = ((2, SPAN, SLIM), BF16)
    made = [
        call(
            functools.partial(state_kernel, g),
            "state" + str(g),
            [slim, slim, group_square, group_square],
            [doc_starts, k, v, kv_got[g]],
            scalars=1,
            flops=mm // GROUPS,
        )
        for g in range(GROUPS)
    ]
    sent = [m[3] for m in made]
    local = call(
        local_kernel,
        "local",
        [rows, ((2, HALF, SPAN, SPAN), BF16), wide_rows],
        [q, qc_got] + [x for m in made for x in m[:2]],
        flops=2 * mm,
    )
    parts, local = arriving(sent, 1, local)
    fq, scores, attn = local
    normed = [
        call(
            functools.partial(norm_kernel, g, len(parts[g])),
            "norm" + str(g),
            [group_pair, ((2, SPAN, SLIM), BF16), group_square, group_square, ((SIZE, DH), F32)],
            [doc_starts, gain, *parts[g], made[g][2], fq, cot, qc_got, attn],
            scalars=1,
            scratch=[pltpu.VMEM((2, SIZE, SPAN, DH), F32)],
            flops=2 * mm // GROUPS,
        )
        for g in range(GROUPS)
    ]
    dp = lax.axis_size("dp")

    def across(x, axis, low, size):
        length = lax.axis_size(axis)

        def other(y, bit):
            return lax.ppermute(y, axis, [(i, i ^ bit) for i in range(length)])

        while size > (4 if axis == "ctx" else 2):
            x, low, size = x + other(x, low), 2 * low, size // 2
        if size == 2:
            return x + other(x, low)
        if size == 4:
            near, side, cross = other(x, low), other(x, 2 * low), other(x, 3 * low)
            return (x + near) + (side + cross)
        return x

    total = across(jnp.concatenate([n[4] for n in normed]), "ctx", 2, chips)
    parts_back, total = arriving([n[2] for n in normed], -1, total)

    queries_out = []
    for g in range(GROUPS):
        states, ag = normed[g][:2]
        fk, vv = made[g][:2]
        queries_out.append(
            call(
                functools.partial(mixed_kernel, g),
                "mixed" + str(g),
                [((SPAN, SLIM), BF16), ((SPAN, SLIM), F32), slim_rows, slim_rows],
                [q, qc_got, ag, vv, fk, fq, scores, states],
                scratch=[pltpu.VMEM((2, SIZE, SPAN, SPAN), BF16)],
                flops=5 * mm // GROUPS,
            )
        )

    def outputs(g):
        fk, vv = made[g][:2]
        extra = [queries_out[g][1]]
        return call(
            functools.partial(final_kernel, g, len(parts_back[g]), len(extra)),
            "final" + str(g),
            [((2, SPAN, SLIM), BF16), ((len(extra) + 2, SPAN, SLIM), F32)],
            [doc_starts, *parts_back[g], *extra, k, kv_got[g], normed[g][3], *queries_out[g][2:], vv, fk],
            scalars=1,
            scratch=[pltpu.VMEM((2, SIZE, DH, DH), BF16)],
            flops=2 * mm // GROUPS,
        )

    done = [outputs(g) for g in range(GROUPS)]
    bit = 1
    while bit < dp:
        got = lax.ppermute(total, "dp", [(i, i ^ bit) for i in range(dp)])
        if bit == 1:
            got, done[-1] = lax.optimization_barrier((got, done[-1]))
        total = total + got
        bit *= 2
    done[0], total = lax.optimization_barrier((done[0], total))
    joined = [x[0] for x in queries_out]
    for own, back in done:
        joined += [own, lax.ppermute(back, "ctx", swap)]
    total_other = lax.ppermute(total, "ctx", swap)
    query_grad, key_grad, value_grad, gain_grad = call(
        functools.partial(join_kernel, dp * SPAN * count),
        "join",
        [((SPAN, H * DH), BF16)] * 3 + [((H, DH), F32)],
        [*joined, total, total_other],
    )
    return query_grad[None], key_grad[None], value_grad[None], gain_grad.reshape(H * DH)


def solution(mesh):
    placed = (
        P("dp", "ctx", None),
        P("dp", "ctx", None),
        P("dp", "ctx", None),
        P("dp", "ctx", None),
        P(),
        P("dp", None),
    )
    return jax.shard_map(
        per_device,
        mesh=mesh,
        in_specs=placed,
        out_specs=(P("dp", "ctx", None), P("dp", "ctx", None), P("dp", "ctx", None), P()),
        check_vma=False,
    )
```

```python
import functools

import jax
import jax.numpy as jnp
from jax import lax
from jax.experimental import pallas as pl
from jax.experimental.pallas import tpu as pltpu
from jax.sharding import PartitionSpec as P

H = 16
DH = 128
SPAN = 128
HALF = H // 2
WIDE = HALF * DH
EPS = 1e-06
GROUPS = 2
SIZE = HALF // GROUPS
SLIM = SIZE * DH

F32 = jnp.float32
BF16 = jnp.bfloat16


def dot(a, b, ca, cb):
    return lax.dot_general(a, b, (((ca,), (cb,)), ((), ())), preferred_element_type=F32)


def phi(x):
    wide = x.astype(F32)
    return jnp.where(wide > 0, wide + 1.0, jnp.exp(jnp.minimum(wide, 0.0)))


def slope(x):
    wide = x.astype(F32)
    return jnp.where(wide > 0, 1.0, jnp.exp(jnp.minimum(wide, 0.0)))


def causal():
    rows = lax.broadcasted_iota(jnp.int32, (SPAN, SPAN), 0)
    cols = lax.broadcasted_iota(jnp.int32, (SPAN, SPAN), 1)
    return cols <= rows


def unflagged(starts_ref, block):
    hit = jnp.logical_or(block <= 0, block >= lax.axis_size("ctx"))
    for d in range(starts_ref.shape[1]):
        hit = jnp.logical_or(hit, starts_ref[0, d] == block)
    return jnp.where(hit, 0.0, 1.0).astype(F32)


def place():
    c = lax.axis_index("ctx")
    j = lax.rem(c, 2)
    return j, c - j


def columns(j, h):
    return pl.ds(pl.multiple_of(j * WIDE + h * DH, DH), DH)


def head(h):
    return slice(h * DH, (h + 1) * DH)


def pack_kernel(pieces, count, *refs):
    j, _ = place()
    ins, outs = refs[:count], refs[count : count + len(pieces)]
    held, sems = refs[count + len(pieces) : -1], refs[-1]
    copies = []
    for p, (pair, start, wide) in enumerate(pieces):
        cols = pl.ds(pl.multiple_of((1 - j) * WIDE + start, DH), wide)
        for side in range(2):
            source = ins[2 * pair + side].at[:, cols]
            copies.append(pltpu.make_async_copy(source, held[p].at[side], sems.at[2 * p + side]))
    for copy in copies:
        copy.start()
    for p in range(len(pieces)):
        for side in range(2):
            copies[2 * p + side].wait()
            outs[p][side] = held[p][side].astype(F32)


def widen_kernel(q_ref, c_ref, out_ref):
    j, _ = place()
    half = pl.ds(pl.multiple_of((1 - j) * WIDE, WIDE), WIDE)
    out_ref[0] = q_ref[:, half].astype(F32)
    out_ref[1] = c_ref[:, half].astype(F32)


def state_kernel(group, starts_ref, k_ref, v_ref, got_ref, fk_ref, vv_ref, first_ref, sent_ref):
    j, z = place()
    inner = unflagged(starts_ref, z + 1)
    lower = j == 0
    for i in range(SIZE):
        cols = columns(j, group * SIZE + i)
        fk_ref[0, :, head(i)] = phi(k_ref[:, cols]).astype(BF16)
        fk_ref[1, :, head(i)] = phi(got_ref[0, :, head(i)]).astype(BF16)
        vv_ref[0, :, head(i)] = v_ref[:, cols]
        vv_ref[1, :, head(i)] = got_ref[1, :, head(i)].astype(BF16)
    for i in range(SIZE):
        own, other = (dot(fk_ref[b, :, head(i)], vv_ref[b, :, head(i)], 0, 0) for b in range(2))
        first = jnp.where(lower, own, other) * inner
        first_ref[i] = first
        sent_ref[i] = jnp.where(lower, other, own) + first


def local_kernel(q_ref, got_ref, *refs):
    features, (fq_ref, scores_ref, attn_ref) = refs[:-3], refs[-3:]
    j, _ = place()
    keep = causal()
    units = [(b, g, i) for b in range(2) for g in range(GROUPS) for i in range(SIZE)]
    for h in range(HALF):
        fq_ref[0, :, head(h)] = phi(q_ref[:, columns(j, h)]).astype(BF16)
        fq_ref[1, :, head(h)] = phi(got_ref[0, :, head(h)]).astype(BF16)
    for b, g, i in units:
        h = g * SIZE + i
        raw = dot(fq_ref[b, :, head(h)], features[2 * g][b, :, head(i)], 1, 1)
        scores_ref[b, h] = jnp.where(keep, raw, 0.0).astype(BF16)
    for b, g, i in units:
        h = g * SIZE + i
        attn_ref[b, :, head(h)] = dot(scores_ref[b, h], features[2 * g + 1][b, :, head(i)], 1, 0)


def weighted(parts, weights, h):
    total = parts[0][h]
    for part, weight in zip(parts[1:], weights):
        total = total + weight * part[h]
    return total


def link_weights(starts_ref, count, nearest, step):
    weights, block, weight = [], nearest, 1.0
    for _ in range(count - 1):
        weight = weight * unflagged(starts_ref, block) * unflagged(starts_ref, block + step)
        weights.append(weight)
        block = block + 2 * step
    return weights


def norm_kernel(group, count, starts_ref, gain_ref, *refs):
    parts, refs = refs[:count], refs[count:]
    first_ref, fq_ref, c_ref, got_ref, attn_ref, state_ref, ag_ref, sent_ref, second_ref, part_ref, whole_ref = refs
    j, z = place()
    outer, inner = unflagged(starts_ref, z), unflagged(starts_ref, z + 1)
    weights = link_weights(starts_ref, count, z - 1, -1)
    lower = j == 0
    units = [(b, i) for i in range(SIZE) for b in range(2)]
    for i in range(SIZE):
        entering = outer * weighted(parts, weights, i)
        inside = inner * entering + first_ref[i]
        state_ref[0, i] = jnp.where(lower, entering, inside).astype(BF16)
        state_ref[1, i] = jnp.where(lower, inside, entering).astype(BF16)
    for b, i in units:
        cols = head(group * SIZE + i)
        whole_ref[b, i] = attn_ref[b, :, cols] + dot(fq_ref[b, :, cols], state_ref[b, i], 1, 0)
    for i in range(SIZE):
        h = group * SIZE + i
        gain = gain_ref[:, columns(j, h)]
        partial = jnp.zeros((1, DH), F32)
        for b in range(2):
            attn = whole_ref[b, i]
            cot = got_ref[1, :, head(h)] if b else c_ref[:, columns(j, h)].astype(F32)
            scaled = gain * cot
            square = jnp.mean(attn * attn, axis=-1, keepdims=True)
            along = jnp.mean(attn * scaled, axis=-1, keepdims=True)
            inverse = lax.rsqrt(square + EPS)
            normed = attn * inverse
            partial = partial + jnp.sum(normed * cot, axis=0, keepdims=True)
            ag_ref[b, :, head(i)] = ((scaled - normed * (along * inverse)) * inverse).astype(BF16)
        part_ref[i : i + 1, :] = partial
    for i in range(SIZE):
        cols = head(group * SIZE + i)
        own, other = (dot(fq_ref[b, :, cols], ag_ref[b, :, head(i)], 0, 0) for b in range(2))
        second = inner * jnp.where(lower, other, own)
        second_ref[i] = second
        sent_ref[i] = jnp.where(lower, own, other) + second


def mixed_kernel(
    group, q_ref, got_ref, ag_ref, vv_ref, fk_ref, fq_ref, scores_ref, state_ref, own_ref, other_ref, kl_ref, vl_ref, mm_ref
):
    j, _ = place()
    keep = causal()
    units = [(b, i) for i in range(SIZE) for b in range(2)]
    for b, i in units:
        raw = dot(ag_ref[b, :, head(i)], vv_ref[b, :, head(i)], 1, 1)
        mm_ref[b, i] = jnp.where(keep, raw, 0.0).astype(BF16)
    for b, i in units:
        vl_ref[b, :, head(i)] = dot(scores_ref[b, group * SIZE + i], ag_ref[b, :, head(i)], 0, 0)
    for b, i in units:
        cols = head(group * SIZE + i)
        part = dot(mm_ref[b, i], fk_ref[b, :, head(i)], 1, 0) + dot(ag_ref[b, :, head(i)], state_ref[b, i], 1, 1)
        if b:
            other_ref[:, head(i)] = part * slope(got_ref[0, :, cols])
        else:
            own_ref[:, head(i)] = (part * slope(q_ref[:, columns(j, group * SIZE + i)])).astype(BF16)
    for b, i in units:
        kl_ref[b, :, head(i)] = dot(mm_ref[b, i], fq_ref[b, :, head(group * SIZE + i)], 0, 0)


def final_kernel(group, count, extras, starts_ref, *refs):
    parts, more, refs = refs[:count], refs[count : count + extras], refs[count + extras :]
    k_ref, got_ref, second_ref, kl_ref, vl_ref, vv_ref, fk_ref, own_ref, other_ref, back_ref = refs
    j, z = place()
    outer, inner = unflagged(starts_ref, z + 2), unflagged(starts_ref, z + 1)
    lower = j == 0
    weights = link_weights(starts_ref, count, z + 3, 1)
    for e in range(extras):
        other_ref[e] = more[e][...]
    for i in range(SIZE):
        entering = outer * weighted(parts, weights, i)
        inside = inner * entering + second_ref[i]
        back_ref[0, i] = jnp.where(lower, inside, entering).astype(BF16)
        back_ref[1, i] = jnp.where(lower, entering, inside).astype(BF16)
    for i in range(SIZE):
        h = group * SIZE + i
        for b in range(2):
            key = kl_ref[b, :, head(i)] + dot(vv_ref[b, :, head(i)], back_ref[b, i], 1, 1)
            value = vl_ref[b, :, head(i)] + dot(fk_ref[b, :, head(i)], back_ref[b, i], 1, 0)
            if b:
                other_ref[extras, :, head(i)] = key * slope(got_ref[0, :, head(i)])
                other_ref[extras + 1, :, head(i)] = value
            else:
                own_ref[0, :, head(i)] = (key * slope(k_ref[:, columns(j, h)])).astype(BF16)
                own_ref[1, :, head(i)] = value.astype(BF16)


def join_kernel(tokens, *refs):
    j, _ = place()
    total_ref, total_got_ref, q_ref, k_ref, v_ref, gain_ref = refs[-6:]
    root = jnp.sqrt(F32(tokens))
    gain_ref[pl.ds(pl.multiple_of(j * HALF, HALF), HALF), :] = total_ref[...] / root
    gain_ref[pl.ds(pl.multiple_of((1 - j) * HALF, HALF), HALF), :] = total_got_ref[...] / root
    for g in range(GROUPS):
        kv_own_ref, kv_got_ref = refs[GROUPS + 2 * g : GROUPS + 2 * g + 2]
        for i in range(SIZE):
            h = g * SIZE + i
            for ref, own, got in (
                (q_ref, refs[g], kv_got_ref.at[0]),
                (k_ref, kv_own_ref.at[0], kv_got_ref.at[1]),
                (v_ref, kv_own_ref.at[1], kv_got_ref.at[2]),
            ):
                ref[:, columns(j, h)] = own[:, head(i)]
                ref[:, columns(1 - j, h)] = got[:, head(i)].astype(BF16)


VM = pl.BlockSpec(memory_space=pltpu.VMEM)
SM = pl.BlockSpec(memory_space=pltpu.SMEM)
HB = pl.BlockSpec(memory_space=pltpu.HBM)


def call(kernel, name, outs, args, scalars=0, whole=(), aliases={}, scratch=(), flops=0):
    moved = sum(a.size * a.dtype.itemsize for a in args) + sum(
        o[0][0] * functools.reduce(lambda x, y: x * y, o[0][1:], 1) * jnp.dtype(o[1]).itemsize for o in outs
    )
    return pl.pallas_call(
        kernel,
        out_shape=[jax.ShapeDtypeStruct(s, d) for s, d in outs],
        in_specs=[SM if i < scalars else HB if i in whole else VM for i in range(len(args))],
        input_output_aliases=aliases,
        out_specs=[VM] * len(outs),
        scratch_shapes=scratch,
        compiler_params=pltpu.CompilerParams(vmem_limit_bytes=24 * 1024 * 1024),
        cost_estimate=pl.CostEstimate(flops=flops, bytes_accessed=moved, transcendentals=0),
        name=name,
    )(*args)


def per_device(queries, key_rows, value_rows, out_cotangent, norm_gain, doc_starts):
    count = lax.axis_size("ctx")
    chips = count // 2
    documents = doc_starts.shape[1]
    swap = [(i, i ^ 1) for i in range(count)]
    reach = min(chips - 1, -(-(count - documents) // 2))
    q, k, v, cot = queries[0], key_rows[0], value_rows[0], out_cotangent[0]
    gain = norm_gain.reshape(1, H * DH)
    mm = 2 * HALF * 2 * SPAN * DH * DH

    def turn(x, distance):
        return lax.ppermute(x, "ctx", [(i, (i + 2 * distance) % count) for i in range(count)])

    def hop(x, distance):
        pairs = [
            (2 * i + j, 2 * (i + distance) + j)
            for i in range(chips)
            for j in range(2)
            if 0 <= i + distance < chips
        ]
        return lax.ppermute(x, "ctx", pairs)

    def arriving(sent, sign, first=None, later=None):
        if reach <= 3:
            parts = [[] for _ in sent]
            for r in range(reach):
                sent = [(turn if (sign > 0) == (r == 0) else hop)(x, sign) for x in sent]
                if r == 0 and first is not None:
                    at = -1 if sign > 0 else 0
                    sent[at], first = lax.optimization_barrier((sent[at], first))
                for group, x in zip(parts, sent):
                    group.append(x)
            return parts, first
        starts = doc_starts[0]
        chip = lax.axis_index("ctx") // 2

        def linked(low, high):
            return 1.0 - jnp.any((starts >= low) & (starts <= high)).astype(F32)

        distance = 1
        while distance < chips:
            if sign > 0:
                weight = linked(2 * (chip - distance) + 2, 2 * chip + 1)
            else:
                weight = linked(2 * chip + 1, 2 * (chip + distance))
            sent = [x + weight * hop(x, sign * distance) for x in sent]
            distance *= 2
        return [[hop(x, sign)] for x in sent], first

    order = list(range(GROUPS))[::-1]
    pieces = [(0, g * SLIM, SLIM) for g in order]
    kv_send = call(
        functools.partial(pack_kernel, pieces, 2),
        "pack",
        [((2, SPAN, wide), F32) for _, _, wide in pieces],
        [pltpu.with_memory_space_constraint(x, pltpu.HBM) for x in (k, v)],
        whole=range(2),
        scratch=[pltpu.VMEM((2, SPAN, wide), BF16) for _, _, wide in pieces]
        + [pltpu.SemaphoreType.DMA((2 * len(pieces),))],
    )
    ahead = lax.ppermute(kv_send[0], "ctx", swap)
    ahead, kv_send, q, cot = lax.optimization_barrier((ahead, kv_send[1:], q, cot))
    (qc_send,) = call(widen_kernel, "widen", [((2, SPAN, WIDE), F32)], [q, cot])
    kv_got = [ahead, *(lax.ppermute(x, "ctx", swap) for x in kv_send)][::-1]
    qc_got = lax.ppermute(qc_send, "ctx", swap)
    mm = 2 * HALF * 2 * SPAN * DH * DH
    rows = ((2, SPAN, WIDE), BF16)
    wide_rows = ((2, SPAN, WIDE), F32)
    slim_rows = ((2, SPAN, SLIM), F32)
    group_square = ((SIZE, DH, DH), F32)
    group_pair = ((2, SIZE, DH, DH), BF16)
    slim = ((2, SPAN, SLIM), BF16)
    made = [
        call(
            functools.partial(state_kernel, g),
            "state" + str(g),
            [slim, slim, group_square, group_square],
            [doc_starts, k, v, kv_got[g]],
            scalars=1,
            flops=mm // GROUPS,
        )
        for g in range(GROUPS)
    ]
    sent = [m[3] for m in made]
    local = call(
        local_kernel,
        "local",
        [rows, ((2, HALF, SPAN, SPAN), BF16), wide_rows],
        [q, qc_got] + [x for m in made for x in m[:2]],
        flops=2 * mm,
    )
    parts, local = arriving(sent, 1, local)
    fq, scores, attn = local
    normed = [
        call(
            functools.partial(norm_kernel, g, len(parts[g])),
            "norm" + str(g),
            [group_pair, ((2, SPAN, SLIM), BF16), group_square, group_square, ((SIZE, DH), F32)],
            [doc_starts, gain, *parts[g], made[g][2], fq, cot, qc_got, attn],
            scalars=1,
            scratch=[pltpu.VMEM((2, SIZE, SPAN, DH), F32)],
            flops=2 * mm // GROUPS,
        )
        for g in range(GROUPS)
    ]
    dp = lax.axis_size("dp")

    def across(x, axis, low, size):
        length = lax.axis_size(axis)

        def other(y, bit):
            return lax.ppermute(y, axis, [(i, i ^ bit) for i in range(length)])

        while size > (4 if axis == "ctx" else 2):
            x, low, size = x + other(x, low), 2 * low, size // 2
        if size == 2:
            return x + other(x, low)
        if size == 4:
            near, side, cross = other(x, low), other(x, 2 * low), other(x, 3 * low)
            return (x + near) + (side + cross)
        return x

    total = across(jnp.concatenate([n[4] for n in normed]), "ctx", 2, chips)
    parts_back, total = arriving([n[2] for n in normed], -1, total)

    queries_out = []
    for g in range(GROUPS):
        states, ag = normed[g][:2]
        fk, vv = made[g][:2]
        queries_out.append(
            call(
                functools.partial(mixed_kernel, g),
                "mixed" + str(g),
                [((SPAN, SLIM), BF16), ((SPAN, SLIM), F32), slim_rows, slim_rows],
                [q, qc_got, ag, vv, fk, fq, scores, states],
                scratch=[pltpu.VMEM((2, SIZE, SPAN, SPAN), BF16)],
                flops=5 * mm // GROUPS,
            )
        )

    def outputs(g):
        fk, vv = made[g][:2]
        extra = [queries_out[g][1]]
        return call(
            functools.partial(final_kernel, g, len(parts_back[g]), len(extra)),
            "final" + str(g),
            [((2, SPAN, SLIM), BF16), ((len(extra) + 2, SPAN, SLIM), F32)],
            [doc_starts, *parts_back[g], *extra, k, kv_got[g], normed[g][3], *queries_out[g][2:], vv, fk],
            scalars=1,
            scratch=[pltpu.VMEM((2, SIZE, DH, DH), BF16)],
            flops=2 * mm // GROUPS,
        )

    done = [outputs(g) for g in range(GROUPS)]
    bit = 1
    while bit < dp:
        got = lax.ppermute(total, "dp", [(i, i ^ bit) for i in range(dp)])
        if bit == 1:
            got, done[-1] = lax.optimization_barrier((got, done[-1]))
        total = total + got
        bit *= 2
    done[0], total = lax.optimization_barrier((done[0], total))
    joined = [x[0] for x in queries_out]
    for own, back in done:
        joined += [own, lax.ppermute(back, "ctx", swap)]
    total_other = lax.ppermute(total, "ctx", swap)
    query_grad, key_grad, value_grad, gain_grad = call(
        functools.partial(join_kernel, dp * SPAN * count),
        "join",
        [((SPAN, H * DH), BF16)] * 3 + [((H, DH), F32)],
        [*joined, total, total_other],
    )
    return query_grad[None], key_grad[None], value_grad[None], gain_grad.reshape(H * DH)


def solution(mesh):
    placed = (
        P("dp", "ctx", None),
        P("dp", "ctx", None),
        P("dp", "ctx", None),
        P("dp", "ctx", None),
        P(),
        P("dp", None),
    )
    return jax.shard_map(
        per_device,
        mesh=mesh,
        in_specs=placed,
        out_specs=(P("dp", "ctx", None), P("dp", "ctx", None), P("dp", "ctx", None), P()),
        check_vma=False,
    )
```
